32 devices in a mesh: row: 16 (over z, x, core), col: 2 (over y).
Axes of the slice: x: 2, y: 2, z: 4, core: 2. Of those that a mesh axis runs over, the one named last changes fastest.
Arguments:
- node_feats: bfloat16 [49152, 512], P(('row', 'col')), may hold values from -6 to 6
- w_msg: bfloat16 [512, 512], replicated, may hold values from -0.25 to 0.25
- step_table: bfloat16 [1000, 512], replicated, may hold values from -3 to 3
- step_ids: int32 [49152], P(('row', 'col')), may hold values from 0 to 999
- tile_vals: bfloat16 [1152, 128, 128], P('row'), may hold values from -0.5 to 0.5
- tile_owner: int32 [1152, 1], P('row'), may hold values from 0 to 15; in each aligned block of 72 rows (0 to 71, 72 to 143, ...) at most 9 rows name the same one
- tile_dst_off: int32 [1152], P('row'), may hold values from 0 to 23
- tile_src: int32 [1152], P('row'), may hold values from 0 to 23
- cotangent: bfloat16 [512, 49152], P('col', 'row'), may hold values from -6 to 6
Outputs:
- aggregated: bfloat16 [512, 49152], P('col', 'row')
- feat_grad: bfloat16 [49152, 512], P(('row', 'col'))
- weight_grad: bfloat16 [512, 512], replicated
The draws below stay inside these ranges and needn't reach their ends.
Inputs may be any that keep to these rules, and one draw needn't show every extreme that they name: `tile_owner`: among the 72 tiles of one index of row, at most 9 name the same owner row index, and some row index reaches 9.
All inputs are finite; a program needn't handle non-finite values.
Results may differ from the reference program's by a relative error of at most 0.012.
Values may be sent and summed in bfloat16 or wider, within the bound.
No kernel may reach another device: no remote copies, remote signals or barrier semaphores. Data moves between devices by JAX's collectives and lax.ppermute only.
A program may use at most 64 MiB of HBM per device.

```python
import math
import jax
import jax.numpy as jnp
import numpy as np
from jax import lax

H = 512
TB = 128
TSTEPS = 1000
BLK = 24
TD = 72
CAP = 9
NODES = 49152
N_ROW = 16


def set_ends(result, key, least, high):
    longest = result.shape.index(max(result.shape))
    spots = []
    for shift in (0, 1):
        where = [jax.random.randint(jax.random.fold_in(key, axis), (), 0, length) for axis, length in enumerate(result.shape)]
        where[longest] = (where[longest] + shift) % result.shape[longest]
        spots.append(tuple(where))
    return result.at[spots[0]].set(least).at[spots[1]].set(high)


def with_spikes(entries, key, source, target, shards_of, factor):
    def block_of(axis_at):
        return (jnp.arange(entries.shape[axis_at]) // (entries.shape[axis_at] // shards_of)).reshape((-1,) + (1,) * (entries.ndim - 1 - axis_at))

    one_side = jax.random.permutation(key, shards_of)[block_of(target)]
    other_side = (block_of(target) + shards_of // 2) % shards_of
    return jnp.where((block_of(source) == one_side) | (block_of(source) == other_side), factor * entries, entries)


def steps_of(rng, extent, cuts, smallest, high):
    factor_of, own = 1.0, jax.random.fold_in(rng, 6)
    for dim, shards_of in cuts:
        draws = jnp.exp(jax.random.uniform(jax.random.fold_in(own, dim), (shards_of,), jnp.float32, smallest / len(cuts), high / len(cuts)))
        factor_of = factor_of * jnp.repeat(draws, extent[dim] // shards_of).reshape([-1 if axis == dim else 1 for axis in range(len(extent))])
    return factor_of


def shared_out(key, own, number, rows, count, top, bound, lean):
    order = jax.random.permutation(key, count)
    heavy_load, usual = load_shares(count, rows * top, bound, lean, True), load_shares(count, rows * top, bound, lean, False)
    places = jnp.arange(count)

    def named(sizes, turn):
        used = int((sizes > 0).sum())
        fixed = max(1, used // 4)
        passed = fixed + (places - fixed + turn * (used - fixed)) % max(1, count - fixed)
        return jnp.zeros((count,), jnp.int32).at[order[jnp.where(places < fixed, places, passed)]].set(jnp.asarray(sizes, jnp.int32))

    sizes = jnp.where(number % 4 == 0, named(heavy_load, number // 4), named(usual, number - number // 4 - 1))
    mixed = jax.random.permutation(jax.random.fold_in(own, 3), count)
    donor, sink = mixed[0:count // 2 * 2:2], mixed[1:count // 2 * 2:2]
    slack = jnp.minimum(sizes[donor] - 1, bound - sizes[sink]) // 2
    slack = jnp.where((donor == order[0]) | (sink == order[0]) | (sizes[sink] == 0), 0, jnp.maximum(slack, 0))
    passed = jax.random.randint(jax.random.fold_in(own, 4), (count // 2,), 0, 1 << 20) % (slack + 1)
    sizes = sizes.at[donor].add(-passed).at[sink].add(passed)
    labels = jnp.searchsorted(jnp.cumsum(sizes), jnp.arange(rows * top), side="right").astype(jnp.int32)
    table = labels.reshape(top, rows).T
    table = table[jax.random.permutation(jax.random.fold_in(own, 1), rows)]
    turn = jax.random.randint(jax.random.fold_in(own, 2), (rows, 1), 0, top)
    return jnp.take_along_axis(table, (jnp.arange(top)[None, :] + turn) % top, axis=1)


def load_shares(number_of, total, most, slope, full):
    loads = [(1 << 20) // math.isqrt(rank ** slope) + 1 for rank in range(1, number_of + 1)]
    largest = most if full else min(most, max(-(-total // number_of), total * loads[0] // sum(loads)))
    least = 1 if total - largest >= number_of - 1 else 0
    counts, rest = [largest] + [least] * (number_of - 1), total - largest - least * (number_of - 1)
    while rest > 0:
        candidates = [i for i in range(1, number_of) if counts[i] < largest] or [i for i in range(1, number_of) if counts[i] < most]
        mass, remaining = sum([loads[i] for i in candidates]), rest
        for i in candidates:
            extra = min(most - counts[i], max(1, remaining * loads[i] // mass), rest)
            counts[i] = counts[i] + extra
            rest = rest - extra
    return np.array(counts)


def noise(stream_key, dims, scale, reach, split=(), kind=jnp.bfloat16):
    factor_of = steps_of(stream_key, dims, split, -0.22, 0.18) if split else 1.0
    array = jax.random.normal(stream_key, dims, jnp.float32) * scale * factor_of
    return jnp.minimum(jnp.maximum(array, -reach), reach).astype(kind)


def noise_with(own_key, shape, deviation, most, cuts, heavy, kind=jnp.bfloat16):
    drawn = deviation * jax.random.normal(own_key, shape, jnp.float32)
    if cuts:
        drawn = drawn * steps_of(own_key, shape, cuts, -0.22, 0.18)
    return jnp.clip(with_spikes(drawn, jax.random.fold_in(own_key, 3), *heavy), -most, most).astype(kind)


def setup_inputs(seed: int = 0) -> dict:
    splits = jax.random.split(jax.random.key(seed), 10)
    node_feats = noise_with(splits[0], (NODES, H), 1.0, 6.0, ((0, 32),), (0, 1, 32, 2.75))
    w_msg = noise(splits[1], (H, H), H ** -0.5, 0.25)
    step_table = noise(splits[2], (TSTEPS, H), 0.5, 3.0)
    step_ids = set_ends(jax.random.randint(splits[3], (NODES,), 0, TSTEPS), jax.random.fold_in(splits[3], 1), 0, TSTEPS - 1).astype(jnp.int32)
    tile_vals = noise(splits[4], (N_ROW * TD, TB, TB), TB ** -0.5, 0.5, ((0, 16),))
    tile_owner_keys = jax.random.split(jax.random.fold_in(splits[5], 1), (N_ROW * TD) // TD)
    tile_owner_turns = jax.random.permutation(jax.random.fold_in(splits[5], 3), (N_ROW * TD) // TD)
    tile_owner = jax.vmap(lambda own, number: shared_out(jax.random.fold_in(splits[5], 2), own, number, TD, N_ROW, 1, CAP, 2))(tile_owner_keys, tile_owner_turns).reshape((N_ROW * TD, 1))
    tile_dst_off = set_ends(jax.random.randint(splits[6], (N_ROW * TD,), 0, BLK), jax.random.fold_in(splits[6], 1), 0, BLK - 1).astype(jnp.int32)
    tile_src = set_ends(jax.random.randint(splits[7], (N_ROW * TD,), 0, BLK), jax.random.fold_in(splits[7], 1), 0, BLK - 1).astype(jnp.int32)
    cotangent = noise(splits[8], (H, NODES), 1.0, 6.0, ((0, 2), (1, 16)))
    return dict(node_feats=node_feats, w_msg=w_msg, step_table=step_table, step_ids=step_ids, tile_vals=tile_vals, tile_owner=tile_owner, tile_dst_off=tile_dst_off, tile_src=tile_src, cotangent=cotangent)


def gelu_value(v):
    return 0.5 * v * (1.0 + jax.scipy.special.erf(v / jnp.sqrt(2.0)))

def gelu_slope(v):
    return 0.5 * (1.0 + jax.scipy.special.erf(v / jnp.sqrt(2.0))) + v * jnp.exp(-0.5 * v * v) / jnp.sqrt(2.0 * jnp.pi)

def reference(node_feats, w_msg, step_table, step_ids, tile_vals, tile_owner, tile_dst_off, tile_src, cotangent):
    pre = jnp.dot(node_feats, w_msg, preferred_element_type=jnp.float32) + step_table[step_ids].astype(jnp.float32)
    msg = gelu_value(pre).astype(jnp.bfloat16)
    msg_blocks = msg.reshape(BLK * N_ROW, TB, H)
    vals = tile_vals.reshape(N_ROW, TD, TB, TB)
    owners = tile_owner.reshape(N_ROW, TD)
    offsets = tile_dst_off.reshape(N_ROW, TD)
    sources = tile_src.reshape(N_ROW, TD)
    rows = jnp.arange(N_ROW, dtype=jnp.int32)

    def fwd_step(agg, items):
        tiles, owner, offset, source, row_idx = items
        src_glob = (row_idx * BLK + source).astype(jnp.int32)
        dst_glob = (owner * BLK + offset).astype(jnp.int32)
        feats = msg_blocks[src_glob].astype(jnp.float32)
        parts = jnp.einsum('tdk,tkf->tdf', tiles.astype(jnp.float32), feats).astype(jnp.bfloat16)
        return (agg.at[dst_glob].add(parts.astype(jnp.float32)), None)
    agg, _ = lax.scan(fwd_step, jnp.zeros((BLK * N_ROW, TB, H), jnp.float32), (vals, owners, offsets, sources, rows))
    aggregated = agg.astype(jnp.bfloat16).reshape(NODES, H).T
    grad_blocks = cotangent.T.reshape(BLK * N_ROW, TB, H)

    def bwd_step(dmsg, items):
        tiles, owner, offset, source, row_idx = items
        src_glob = (row_idx * BLK + source).astype(jnp.int32)
        dst_glob = (owner * BLK + offset).astype(jnp.int32)
        grads = grad_blocks[dst_glob].astype(jnp.float32)
        term = jnp.einsum('tdk,tdf->tkf', tiles.astype(jnp.float32), grads)
        return (dmsg.at[src_glob].add(term), None)
    dmsg, _ = lax.scan(bwd_step, jnp.zeros((BLK * N_ROW, TB, H), jnp.float32), (vals, owners, offsets, sources, rows))
    dmsg = dmsg.astype(jnp.bfloat16).reshape(NODES, H)
    dpre = (dmsg.astype(jnp.float32) * gelu_slope(pre)).astype(jnp.bfloat16)
    feat_grad = jnp.dot(dpre, w_msg.T, preferred_element_type=jnp.float32).astype(jnp.bfloat16)
    weight_grad = jnp.dot(node_feats.T, dpre, preferred_element_type=jnp.float32).astype(jnp.bfloat16)
    return (aggregated, feat_grad, weight_grad)
```

```python
import functools

import jax
import jax.numpy as jnp
import numpy as np
from jax import lax
from jax.experimental import pallas as pl
from jax.experimental.pallas import tpu as pltpu
from jax.sharding import PartitionSpec as P


F32 = jnp.float32
BF16 = jnp.bfloat16
VMEM_LIMIT = 48 * 1024 * 1024


def gelu_value(v):
    return 0.5 * v * (1.0 + jax.scipy.special.erf(v / jnp.sqrt(2.0)))


def gelu_slope(v):
    return 0.5 * (1.0 + jax.scipy.special.erf(v / jnp.sqrt(2.0))) + v * jnp.exp(
        -0.5 * v * v
    ) / jnp.sqrt(2.0 * jnp.pi)


def ring_order(row_count):
    chips = row_count // 2
    bits = max(chips.bit_length() - 1, 0)
    nz = 1 << ((bits + 1) // 2)
    nx = chips // nz
    path = []
    for x in range(nx):
        zs = range(1, nz) if x % 2 == 0 else range(nz - 1, 0, -1)
        if nz == 1:
            zs = range(0)
        path += [(z, x) for z in zs]
    path += [(0, x) for x in range(nx - 1, -1, -1)]
    order = []
    for z, x in path:
        order += [(z * nx + x) * 2, (z * nx + x) * 2 + 1]
    return order


def add_tiles(acc_ref, row, owner, off, src, msg_ref, tiles_ref, side):
    per_part = msg_ref.shape[2] // side

    def step(t, carry):
        @pl.when(owner[t] == row)
        def _():
            s = src[t]
            col = pl.multiple_of(lax.rem(s, per_part) * side, side)
            feats = msg_ref[lax.div(s, per_part), :, pl.ds(col, side)]
            part = lax.dot_general(
                feats, tiles_ref[t], (((1,), (1,)), ((), ())), preferred_element_type=F32
            )
            at = pl.ds(pl.multiple_of(off[t] * side, side), side)
            acc_ref[:, at] = acc_ref[:, at] + part

        return carry

    lax.fori_loop(0, tiles_ref.shape[0], step, 0)


def hop_kernel(which, has_recv, side, rows, owner, off, src, *refs):
    if has_recv:
        recv_ref, msg_ref, tiles_ref, _, out_ref, acc_ref = refs
        acc_ref[...] = recv_ref[...].astype(F32)
    else:
        msg_ref, tiles_ref, _, out_ref, acc_ref = refs
        acc_ref[...] = jnp.zeros_like(acc_ref)
    add_tiles(acc_ref, rows[which], owner, off, src, msg_ref, tiles_ref, side)
    out_ref[...] = acc_ref[...].astype(out_ref.dtype)


def hop(which, half, recv, rows, owner, off, src, msg, tiles, gate, width):
    parts, feats, part_nodes = msg.shape
    fh = feats // 2
    side = tiles.shape[1]
    args = ([recv] if recv is not None else []) + [msg, tiles, gate]
    vm = pl.BlockSpec(memory_space=pltpu.VMEM)
    full = pl.BlockSpec((fh, width), lambda i, *_: (0, 0))
    specs = ([full] if recv is not None else []) + [
        pl.BlockSpec((parts, fh, part_nodes), lambda i, *_: (0, half, 0)),
        pl.BlockSpec(tiles.shape, lambda i, *_: (0, 0, 0)),
        pl.BlockSpec(memory_space=pl.ANY),
    ]
    return pl.pallas_call(
        functools.partial(hop_kernel, which, recv is not None, side),
        out_shape=jax.ShapeDtypeStruct((fh, width), BF16),
        grid_spec=pltpu.PrefetchScalarGridSpec(
            num_scalar_prefetch=4,
            grid=(1,),
            in_specs=specs,
            out_specs=full,
            scratch_shapes=[pltpu.VMEM((fh, width), F32)],
        ),
        compiler_params=pltpu.CompilerParams(vmem_limit_bytes=VMEM_LIMIT),
        cost_estimate=pl.CostEstimate(
            flops=2 * fh * side * side * 9, bytes_accessed=6 * 2**20, transcendentals=0
        ),
        name="hop",
    )(rows, owner, off, src, *args)


def last_kernel(which, side, rows, owner, off, src, p0, m0, p1, m1, msg_ref, tiles_ref, out_ref, acc_ref):
    fh = p0.shape[0]
    acc_ref[:fh, :] = p0[...].astype(F32) + m0[...].astype(F32)
    acc_ref[fh:, :] = p1[...].astype(F32) + m1[...].astype(F32)
    add_tiles(acc_ref, rows[which], owner, off, src, msg_ref, tiles_ref, side)
    out_ref[...] = acc_ref[...].astype(out_ref.dtype)


def last_hop(which, recvs, rows, owner, off, src, msg, tiles, width):
    parts, feats, part_nodes = msg.shape
    side = tiles.shape[1]
    half = pl.BlockSpec((feats // 2, width), lambda i, *_: (0, 0))
    return pl.pallas_call(
        functools.partial(last_kernel, which, side),
        out_shape=jax.ShapeDtypeStruct((feats, width), BF16),
        grid_spec=pltpu.PrefetchScalarGridSpec(
            num_scalar_prefetch=4,
            grid=(1,),
            in_specs=[half] * 4
            + [
                pl.BlockSpec(msg.shape, lambda i, *_: (0, 0, 0)),
                pl.BlockSpec(tiles.shape, lambda i, *_: (0, 0, 0)),
            ],
            out_specs=pl.BlockSpec((feats, width), lambda i, *_: (0, 0)),
            scratch_shapes=[pltpu.VMEM((feats, width), F32)],
        ),
        compiler_params=pltpu.CompilerParams(vmem_limit_bytes=VMEM_LIMIT),
        name="last_hop",
    )(rows, owner, off, src, *recvs, msg, tiles)


def back_kernel(side, owner, off, src, grads_ref, tiles_ref, out_ref, buf_ref, acc_ref, sem):
    count = tiles_ref.shape[0]
    per_part = out_ref.shape[2] // side

    def fetch(t):
        at = pl.ds(pl.multiple_of(off[t] * side, side), side)
        return pltpu.make_async_copy(grads_ref.at[owner[t], :, at], buf_ref.at[t], sem.at[t])

    def begin(t, carry):
        fetch(t).start()
        return carry

    lax.fori_loop(0, count, begin, 0)
    acc_ref[...] = jnp.zeros_like(acc_ref)

    def step(t, carry):
        fetch(t).wait()
        term = jnp.dot(buf_ref[t], tiles_ref[t], preferred_element_type=F32)
        s = src[t]
        at = pl.ds(pl.multiple_of(lax.rem(s, per_part) * side, side), side)
        part = lax.div(s, per_part)
        acc_ref[part, :, at] = acc_ref[part, :, at] + term
        return carry

    lax.fori_loop(0, count, step, 0)
    out_ref[...] = acc_ref[...].astype(out_ref.dtype)


def back(owner, off, src, grads, tiles, parts):
    _, feats, width = grads.shape
    count, side, _ = tiles.shape
    shape = (parts, feats, width // parts)
    return pl.pallas_call(
        functools.partial(back_kernel, side),
        out_shape=jax.ShapeDtypeStruct(shape, BF16),
        grid_spec=pltpu.PrefetchScalarGridSpec(
            num_scalar_prefetch=3,
            grid=(1,),
            in_specs=[
                pl.BlockSpec(memory_space=pl.ANY),
                pl.BlockSpec(tiles.shape, lambda i, *_: (0, 0, 0)),
            ],
            out_specs=pl.BlockSpec(shape, lambda i, *_: (0, 0, 0)),
            scratch_shapes=[
                pltpu.VMEM((count, feats, side), BF16),
                pltpu.VMEM(shape, F32),
                pltpu.SemaphoreType.DMA((count,)),
            ],
        ),
        compiler_params=pltpu.CompilerParams(vmem_limit_bytes=VMEM_LIMIT),
        cost_estimate=pl.CostEstimate(
            flops=2 * feats * side * side * count, bytes_accessed=30 * 2**20, transcendentals=0
        ),
        name="back",
    )(owner, off, src, grads, tiles)


def per_device(
    node_feats,
    w_msg,
    step_table,
    step_ids,
    tile_vals,
    tile_owner,
    tile_dst_off,
    tile_src,
    cotangent,
):
    row_count = lax.axis_size("row")
    col_count = lax.axis_size("col")
    feats, width = cotangent.shape
    owner = tile_owner[:, 0]

    ring = ring_order(row_count)
    pos_of = np.argsort(np.array(ring))
    up = [(ring[p], ring[(p + 1) % row_count]) for p in range(row_count)]
    down = [(b, a) for a, b in up]
    far, near = row_count // 2, row_count - 1 - row_count // 2
    chains = [
        (0, 1, far),
        (0, -1, near),
        (1, 1, near),
        (1, -1, far),
    ]
    table = []
    for half, sign, hops in chains:
        for s in range(hops):
            table.append([ring[(pos_of[r] + sign * (hops - s)) % row_count] for r in range(row_count)])
    table.append(list(range(row_count)))
    table = jnp.asarray(np.array(table, dtype=np.int32).T)
    rows = lax.dynamic_index_in_dim(table, lax.axis_index("row"), 0, keepdims=False)

    grads = lax.all_gather(cotangent, "row", axis=0)

    step_hot = (
        step_ids[:, None] == jnp.arange(step_table.shape[0], dtype=jnp.int32)[None, :]
    ).astype(BF16)
    dims = (((0,), (1,)), ((), ()))
    pre_t = lax.dot_general(w_msg, node_feats, dims, preferred_element_type=F32)
    pre_t = pre_t + lax.dot_general(step_table, step_hot, dims, preferred_element_type=F32)
    msg_t = gelu_value(pre_t).astype(BF16)
    nodes = msg_t.shape[1]
    msg = lax.all_to_all(
        msg_t.reshape(col_count, feats, nodes), "col", split_axis=0, concat_axis=0, tiled=True
    )

    held = [None] * len(chains)
    index = 0
    first = [sum(c[2] for c in chains[:i]) for i in range(len(chains))]
    for s in range(far):
        for i, (half, sign, hops) in enumerate(chains):
            skip = far - hops
            if s < skip:
                continue
            k = s - skip
            out = hop(
                first[i] + k, half, held[i], rows, owner, tile_dst_off, tile_src, msg, tile_vals, grads, width
            )
            held[i] = lax.ppermute(out, "row", up if sign > 0 else down)
    which = sum(c[2] for c in chains)
    aggregated = last_hop(
        which, held, rows, owner, tile_dst_off, tile_src, msg, tile_vals, width
    )

    dmsg = back(owner, tile_dst_off, tile_src, grads, tile_vals, col_count)
    dmsg_rows = lax.all_to_all(dmsg, "col", split_axis=0, concat_axis=0, tiled=True)
    dmsg_rows = dmsg_rows.reshape(col_count * feats, nodes)
    dpre_t = (dmsg_rows.astype(F32) * gelu_slope(pre_t)).astype(BF16)
    feat_grad = lax.dot_general(dpre_t, w_msg, dims, preferred_element_type=F32).astype(BF16)
    weight_term = lax.dot_general(
        node_feats, dpre_t, dims, preferred_element_type=F32
    ).astype(BF16)
    devices = row_count * col_count
    hidden = weight_term.shape[0]
    shares = lax.all_to_all(
        weight_term.reshape(devices, hidden // devices, hidden),
        ("row", "col"),
        split_axis=0,
        concat_axis=0,
        tiled=True,
    )
    share = jnp.sum(shares.astype(F32), axis=0).astype(BF16)
    weight_grad = lax.all_gather(share, ("row", "col"), axis=0, tiled=True)
    return (aggregated, feat_grad, weight_grad)


def solution(mesh):
    return jax.shard_map(
        per_device,
        mesh=mesh,
        in_specs=(
            P(("row", "col"), None),
            P(),
            P(),
            P(("row", "col")),
            P("row", None, None),
            P("row", None),
            P("row"),
            P("row"),
            P("col", "row"),
        ),
        out_specs=(P("col", "row"), P(("row", "col"), None), P()),
        check_vma=False,
    )
```

```python
import functools

import jax
import jax.numpy as jnp
import numpy as np
from jax import lax
from jax.experimental import pallas as pl
from jax.experimental.pallas import tpu as pltpu
from jax.sharding import PartitionSpec as P


F32 = jnp.float32
BF16 = jnp.bfloat16
VMEM_LIMIT = 48 * 1024 * 1024


def gelu_value(v):
    return 0.5 * v * (1.0 + jax.scipy.special.erf(v / jnp.sqrt(2.0)))


def gelu_slope(v):
    return 0.5 * (1.0 + jax.scipy.special.erf(v / jnp.sqrt(2.0))) + v * jnp.exp(
        -0.5 * v * v
    ) / jnp.sqrt(2.0 * jnp.pi)


def ring_order(row_count):
    chips = row_count // 2
    bits = max(chips.bit_length() - 1, 0)
    nz = 1 << ((bits + 1) // 2)
    nx = chips // nz
    path = []
    for x in range(nx):
        zs = range(1, nz) if x % 2 == 0 else range(nz - 1, 0, -1)
        if nz == 1:
            zs = range(0)
        path += [(z, x) for z in zs]
    path += [(0, x) for x in range(nx - 1, -1, -1)]
    order = []
    for z, x in path:
        order += [(z * nx + x) * 2, (z * nx + x) * 2 + 1]
    return order


def add_tiles(acc_ref, row, owner, off, src, msg_ref, tiles_ref, side):
    per_part = msg_ref.shape[2] // side

    def step(t, carry):
        @pl.when(owner[t] == row)
        def _():
            s = src[t]
            col = pl.multiple_of(lax.rem(s, per_part) * side, side)
            feats = msg_ref[lax.div(s, per_part), :, pl.ds(col, side)]
            part = lax.dot_general(
                feats, tiles_ref[t], (((1,), (1,)), ((), ())), preferred_element_type=F32
            )
            at = pl.ds(pl.multiple_of(off[t] * side, side), side)
            acc_ref[:, at] = acc_ref[:, at] + part

        return carry

    lax.fori_loop(0, tiles_ref.shape[0], step, 0)


def hop_kernel(which, has_recv, side, rows, owner, off, src, *refs):
    if has_recv:
        recv_ref, msg_ref, tiles_ref, _, out_ref, acc_ref = refs
        acc_ref[...] = recv_ref[...].astype(F32)
    else:
        msg_ref, tiles_ref, _, out_ref, acc_ref = refs
        acc_ref[...] = jnp.zeros_like(acc_ref)
    add_tiles(acc_ref, rows[which], owner, off, src, msg_ref, tiles_ref, side)
    out_ref[...] = acc_ref[...].astype(out_ref.dtype)


def hop(which, half, recv, rows, owner, off, src, msg, tiles, gate, width):
    parts, feats, part_nodes = msg.shape
    fh = feats // 2
    side = tiles.shape[1]
    args = ([recv] if recv is not None else []) + [msg, tiles, gate]
    vm = pl.BlockSpec(memory_space=pltpu.VMEM)
    full = pl.BlockSpec((fh, width), lambda i, *_: (0, 0))
    specs = ([full] if recv is not None else []) + [
        pl.BlockSpec((parts, fh, part_nodes), lambda i, *_: (0, half, 0)),
        pl.BlockSpec(tiles.shape, lambda i, *_: (0, 0, 0)),
        pl.BlockSpec(memory_space=pl.ANY),
    ]
    return pl.pallas_call(
        functools.partial(hop_kernel, which, recv is not None, side),
        out_shape=jax.ShapeDtypeStruct((fh, width), BF16),
        grid_spec=pltpu.PrefetchScalarGridSpec(
            num_scalar_prefetch=4,
            grid=(1,),
            in_specs=specs,
            out_specs=full,
            scratch_shapes=[pltpu.VMEM((fh, width), F32)],
        ),
        compiler_params=pltpu.CompilerParams(vmem_limit_bytes=VMEM_LIMIT),
        cost_estimate=pl.CostEstimate(
            flops=2 * fh * side * side * 9, bytes_accessed=6 * 2**20, transcendentals=0
        ),
        name="hop",
    )(rows, owner, off, src, *args)


def last_kernel(which, side, rows, owner, off, src, p0, m0, p1, m1, msg_ref, tiles_ref, out_ref, acc_ref):
    fh = p0.shape[0]
    acc_ref[:fh, :] = p0[...].astype(F32) + m0[...].astype(F32)
    acc_ref[fh:, :] = p1[...].astype(F32) + m1[...].astype(F32)
    add_tiles(acc_ref, rows[which], owner, off, src, msg_ref, tiles_ref, side)
    out_ref[...] = acc_ref[...].astype(out_ref.dtype)


def last_hop(which, recvs, rows, owner, off, src, msg, tiles, width):
    parts, feats, part_nodes = msg.shape
    side = tiles.shape[1]
    half = pl.BlockSpec((feats // 2, width), lambda i, *_: (0, 0))
    return pl.pallas_call(
        functools.partial(last_kernel, which, side),
        out_shape=jax.ShapeDtypeStruct((feats, width), BF16),
        grid_spec=pltpu.PrefetchScalarGridSpec(
            num_scalar_prefetch=4,
            grid=(1,),
            in_specs=[half] * 4
            + [
                pl.BlockSpec(msg.shape, lambda i, *_: (0, 0, 0)),
                pl.BlockSpec(tiles.shape, lambda i, *_: (0, 0, 0)),
            ],
            out_specs=pl.BlockSpec((feats, width), lambda i, *_: (0, 0)),
            scratch_shapes=[pltpu.VMEM((feats, width), F32)],
        ),
        compiler_params=pltpu.CompilerParams(vmem_limit_bytes=VMEM_LIMIT),
        name="last_hop",
    )(rows, owner, off, src, *recvs, msg, tiles)


def back_kernel(side, owner, off, src, grads_ref, tiles_ref, *refs):
    out_ref, buf_ref, acc_ref, sem = refs[-4:]
    count = tiles_ref.shape[0]
    per_part = out_ref.shape[2] // side

    def fetch(t):
        at = pl.ds(pl.multiple_of(off[t] * side, side), side)
        return pltpu.make_async_copy(grads_ref.at[owner[t], :, at], buf_ref.at[t], sem.at[t])

    def begin(t, carry):
        fetch(t).start()
        return carry

    lax.fori_loop(0, count, begin, 0)
    acc_ref[...] = jnp.zeros_like(acc_ref)

    def step(t, carry):
        fetch(t).wait()
        term = jnp.dot(buf_ref[t], tiles_ref[t], preferred_element_type=F32)
        s = src[t]
        at = pl.ds(pl.multiple_of(lax.rem(s, per_part) * side, side), side)
        part = lax.div(s, per_part)
        acc_ref[part, :, at] = acc_ref[part, :, at] + term
        return carry

    lax.fori_loop(0, count, step, 0)
    out_ref[...] = acc_ref[...].astype(out_ref.dtype)


def back(owner, off, src, grads, tiles, parts, after):
    _, feats, width = grads.shape
    count, side, _ = tiles.shape
    shape = (parts, feats, width // parts)
    return pl.pallas_call(
        functools.partial(back_kernel, side),
        out_shape=jax.ShapeDtypeStruct(shape, BF16),
        grid_spec=pltpu.PrefetchScalarGridSpec(
            num_scalar_prefetch=3,
            grid=(1,),
            in_specs=[
                pl.BlockSpec(memory_space=pl.ANY),
                pl.BlockSpec(tiles.shape, lambda i, *_: (0, 0, 0)),
            ]
            + [pl.BlockSpec(memory_space=pl.ANY)] * len(after),
            out_specs=pl.BlockSpec(shape, lambda i, *_: (0, 0, 0)),
            scratch_shapes=[
                pltpu.VMEM((count, feats, side), BF16),
                pltpu.VMEM(shape, F32),
                pltpu.SemaphoreType.DMA((count,)),
            ],
        ),
        compiler_params=pltpu.CompilerParams(vmem_limit_bytes=VMEM_LIMIT),
        cost_estimate=pl.CostEstimate(
            flops=2 * feats * side * side * count, bytes_accessed=30 * 2**20, transcendentals=0
        ),
        name="back",
    )(owner, off, src, grads, tiles, *after)


def per_device(
    node_feats,
    w_msg,
    step_table,
    step_ids,
    tile_vals,
    tile_owner,
    tile_dst_off,
    tile_src,
    cotangent,
):
    row_count = lax.axis_size("row")
    col_count = lax.axis_size("col")
    feats, width = cotangent.shape
    owner = tile_owner[:, 0]

    ring = ring_order(row_count)
    pos_of = np.argsort(np.array(ring))
    up = [(ring[p], ring[(p + 1) % row_count]) for p in range(row_count)]
    down = [(b, a) for a, b in up]
    far, near = row_count // 2, row_count - 1 - row_count // 2
    chains = [
        (0, 1, far),
        (0, -1, near),
        (1, 1, near),
        (1, -1, far),
    ]
    table = []
    for half, sign, hops in chains:
        for s in range(hops):
            table.append([ring[(pos_of[r] + sign * (hops - s)) % row_count] for r in range(row_count)])
    table.append(list(range(row_count)))
    table = jnp.asarray(np.array(table, dtype=np.int32).T)
    rows = lax.dynamic_index_in_dim(table, lax.axis_index("row"), 0, keepdims=False)

    grads = lax.all_gather(cotangent, "row", axis=0)

    step_hot = (
        step_ids[:, None] == jnp.arange(step_table.shape[0], dtype=jnp.int32)[None, :]
    ).astype(BF16)
    dims = (((0,), (1,)), ((), ()))
    pre_t = lax.dot_general(w_msg, node_feats, dims, preferred_element_type=F32)
    pre_t = pre_t + lax.dot_general(step_table, step_hot, dims, preferred_element_type=F32)
    msg_t = gelu_value(pre_t).astype(BF16)
    pre_t = lax.optimization_barrier(pre_t)
    nodes = msg_t.shape[1]
    msg = lax.all_to_all(
        msg_t.reshape(col_count, feats, nodes), "col", split_axis=0, concat_axis=0, tiled=True
    )

    held = [None] * len(chains)
    begun = []
    first = [sum(c[2] for c in chains[:i]) for i in range(len(chains))]
    for s in range(far):
        for i, (half, sign, hops) in enumerate(chains):
            skip = far - hops
            if s < skip:
                continue
            k = s - skip
            out = hop(
                first[i] + k, half, held[i], rows, owner, tile_dst_off, tile_src, msg, tile_vals, grads, width
            )
            if s == 0:
                begun.append(out)
            held[i] = lax.ppermute(out, "row", up if sign > 0 else down)
    which = sum(c[2] for c in chains)
    aggregated = last_hop(
        which, held, rows, owner, tile_dst_off, tile_src, msg, tile_vals, width
    )

    dmsg = back(owner, tile_dst_off, tile_src, grads, tile_vals, col_count, begun)
    dmsg_rows = lax.all_to_all(dmsg, "col", split_axis=0, concat_axis=0, tiled=True)
    dmsg_rows = dmsg_rows.reshape(col_count * feats, nodes)
    dpre_t = (dmsg_rows.astype(F32) * gelu_slope(pre_t)).astype(BF16)
    feat_grad = lax.dot_general(dpre_t, w_msg, dims, preferred_element_type=F32).astype(BF16)
    weight_term = lax.dot_general(
        node_feats, dpre_t, dims, preferred_element_type=F32
    ).astype(BF16)
    devices = row_count * col_count
    hidden = weight_term.shape[0]
    shares = lax.all_to_all(
        weight_term.reshape(devices, hidden // devices, hidden),
        ("row", "col"),
        split_axis=0,
        concat_axis=0,
        tiled=True,
    )
    share = jnp.sum(shares.astype(F32), axis=0).astype(BF16)
    weight_grad = lax.all_to_all(
        jnp.broadcast_to(share[None], (devices,) + share.shape),
        ("row", "col"),
        split_axis=0,
        concat_axis=0,
        tiled=True,
    ).reshape(hidden, hidden)
    return (aggregated, feat_grad, weight_grad)


def solution(mesh):
    return jax.shard_map(
        per_device,
        mesh=mesh,
        in_specs=(
            P(("row", "col"), None),
            P(),
            P(),
            P(("row", "col")),
            P("row", None, None),
            P("row", None),
            P("row"),
            P("row"),
            P("col", "row"),
        ),
        out_specs=(P("col", "row"), P(("row", "col"), None), P()),
        check_vma=False,
    )
```

```python
import functools

import jax
import jax.numpy as jnp
import numpy as np
from jax import lax
from jax.experimental import pallas as pl
from jax.experimental.pallas import tpu as pltpu
from jax.sharding import PartitionSpec as P


F32 = jnp.float32
BF16 = jnp.bfloat16
VMEM_LIMIT = 48 * 1024 * 1024
GRID_VMEM = 40 * 1024 * 1024


def gelu_value(v):
    return 0.5 * v * (1.0 + jax.scipy.special.erf(v / jnp.sqrt(2.0)))


def gelu_slope(v):
    return 0.5 * (1.0 + jax.scipy.special.erf(v / jnp.sqrt(2.0))) + v * jnp.exp(
        -0.5 * v * v
    ) / jnp.sqrt(2.0 * jnp.pi)


def ring_order(row_count):
    chips = row_count // 2
    bits = max(chips.bit_length() - 1, 0)
    nz = 1 << ((bits + 1) // 2)
    nx = chips // nz
    path = []
    for x in range(nx):
        zs = range(1, nz) if x % 2 == 0 else range(nz - 1, 0, -1)
        if nz == 1:
            zs = range(0)
        path += [(z, x) for z in zs]
    path += [(0, x) for x in range(nx - 1, -1, -1)]
    order = []
    for z, x in path:
        order += [(z * nx + x) * 2, (z * nx + x) * 2 + 1]
    return order


def add_tiles(acc_ref, row, owner, off, src, msg_ref, tiles_ref, side):
    per_part = msg_ref.shape[2] // side

    def step(t, carry):
        @pl.when(owner[t] == row)
        def _():
            s = src[t]
            col = pl.multiple_of(lax.rem(s, per_part) * side, side)
            feats = msg_ref[lax.div(s, per_part), :, pl.ds(col, side)]
            part = lax.dot_general(
                feats, tiles_ref[t], (((1,), (1,)), ((), ())), preferred_element_type=F32
            )
            at = pl.ds(pl.multiple_of(off[t] * side, side), side)
            acc_ref[:, at] = acc_ref[:, at] + part

        return carry

    lax.fori_loop(0, tiles_ref.shape[0], step, 0)


def hop_kernel(which, has_recv, side, rows, owner, off, src, *refs):
    if has_recv:
        recv_ref, msg_ref, tiles_ref, _, out_ref, acc_ref = refs
        acc_ref[...] = recv_ref[...].astype(F32)
    else:
        msg_ref, tiles_ref, _, out_ref, acc_ref = refs
        acc_ref[...] = jnp.zeros_like(acc_ref)
    add_tiles(acc_ref, rows[which], owner, off, src, msg_ref, tiles_ref, side)
    out_ref[...] = acc_ref[...].astype(out_ref.dtype)


def hop(which, half, recv, rows, owner, off, src, msg, tiles, gate, width):
    parts, feats, part_nodes = msg.shape
    fh = feats // 2
    side = tiles.shape[1]
    args = ([recv] if recv is not None else []) + [msg, tiles, gate]
    vm = pl.BlockSpec(memory_space=pltpu.VMEM)
    full = pl.BlockSpec((fh, width), lambda i, *_: (0, 0))
    specs = ([full] if recv is not None else []) + [
        pl.BlockSpec((parts, fh, part_nodes), lambda i, *_: (0, half, 0)),
        pl.BlockSpec(tiles.shape, lambda i, *_: (0, 0, 0)),
        pl.BlockSpec(memory_space=pl.ANY),
    ]
    return pl.pallas_call(
        functools.partial(hop_kernel, which, recv is not None, side),
        out_shape=jax.ShapeDtypeStruct((fh, width), BF16),
        grid_spec=pltpu.PrefetchScalarGridSpec(
            num_scalar_prefetch=4,
            grid=(1,),
            in_specs=specs,
            out_specs=full,
            scratch_shapes=[pltpu.VMEM((fh, width), F32)],
        ),
        compiler_params=pltpu.CompilerParams(vmem_limit_bytes=VMEM_LIMIT),
        cost_estimate=pl.CostEstimate(
            flops=2 * fh * side * side * 9, bytes_accessed=6 * 2**20, transcendentals=0
        ),
        name="hop",
    )(rows, owner, off, src, *args)


def last_kernel(which, side, rows, owner, off, src, p0, m0, p1, m1, msg_ref, tiles_ref, out_ref, acc_ref):
    fh = p0.shape[0]
    acc_ref[:fh, :] = p0[...].astype(F32) + m0[...].astype(F32)
    acc_ref[fh:, :] = p1[...].astype(F32) + m1[...].astype(F32)
    add_tiles(acc_ref, rows[which], owner, off, src, msg_ref, tiles_ref, side)
    out_ref[...] = acc_ref[...].astype(out_ref.dtype)


def last_hop(which, recvs, rows, owner, off, src, msg, tiles, width):
    parts, feats, part_nodes = msg.shape
    side = tiles.shape[1]
    half = pl.BlockSpec((feats // 2, width), lambda i, *_: (0, 0))
    return pl.pallas_call(
        functools.partial(last_kernel, which, side),
        out_shape=jax.ShapeDtypeStruct((feats, width), BF16),
        grid_spec=pltpu.PrefetchScalarGridSpec(
            num_scalar_prefetch=4,
            grid=(1,),
            in_specs=[half] * 4
            + [
                pl.BlockSpec(msg.shape, lambda i, *_: (0, 0, 0)),
                pl.BlockSpec(tiles.shape, lambda i, *_: (0, 0, 0)),
            ],
            out_specs=pl.BlockSpec((feats, width), lambda i, *_: (0, 0)),
            scratch_shapes=[pltpu.VMEM((feats, width), F32)],
        ),
        compiler_params=pltpu.CompilerParams(vmem_limit_bytes=VMEM_LIMIT),
        name="last_hop",
    )(rows, owner, off, src, *recvs, msg, tiles)


def back_kernel(side, owner, off, src, grads_ref, tiles_ref, *refs):
    out_ref, buf_ref, acc_ref, sem = refs[-4:]
    count = tiles_ref.shape[0]
    per_part = out_ref.shape[2] // side

    def fetch(t):
        at = pl.ds(pl.multiple_of(off[t] * side, side), side)
        return pltpu.make_async_copy(grads_ref.at[owner[t], :, at], buf_ref.at[t], sem.at[t])

    def begin(t, carry):
        fetch(t).start()
        return carry

    lax.fori_loop(0, count, begin, 0)
    acc_ref[...] = jnp.zeros_like(acc_ref)

    def step(t, carry):
        fetch(t).wait()
        term = jnp.dot(buf_ref[t], tiles_ref[t], preferred_element_type=F32)
        s = src[t]
        at = pl.ds(pl.multiple_of(lax.rem(s, per_part) * side, side), side)
        part = lax.div(s, per_part)
        acc_ref[part, :, at] = acc_ref[part, :, at] + term
        return carry

    lax.fori_loop(0, count, step, 0)
    out_ref[...] = acc_ref[...].astype(out_ref.dtype)


def back(owner, off, src, grads, tiles, parts, after):
    _, feats, width = grads.shape
    count, side, _ = tiles.shape
    shape = (parts, feats, width // parts)
    return pl.pallas_call(
        functools.partial(back_kernel, side),
        out_shape=jax.ShapeDtypeStruct(shape, BF16),
        grid_spec=pltpu.PrefetchScalarGridSpec(
            num_scalar_prefetch=3,
            grid=(1,),
            in_specs=[
                pl.BlockSpec(memory_space=pl.ANY),
                pl.BlockSpec(tiles.shape, lambda i, *_: (0, 0, 0)),
            ]
            + [pl.BlockSpec(memory_space=pl.ANY)] * len(after),
            out_specs=pl.BlockSpec(shape, lambda i, *_: (0, 0, 0)),
            scratch_shapes=[
                pltpu.VMEM((count, feats, side), BF16),
                pltpu.VMEM(shape, F32),
                pltpu.SemaphoreType.DMA((count,)),
            ],
        ),
        compiler_params=pltpu.CompilerParams(vmem_limit_bytes=VMEM_LIMIT),
        cost_estimate=pl.CostEstimate(
            flops=2 * feats * side * side * count, bytes_accessed=30 * 2**20, transcendentals=0
        ),
        name="back",
    )(owner, off, src, grads, tiles, *after)


def ring_device(
    node_feats,
    w_msg,
    step_table,
    step_ids,
    tile_vals,
    tile_owner,
    tile_dst_off,
    tile_src,
    cotangent,
):
    row_count = lax.axis_size("row")
    col_count = lax.axis_size("col")
    feats, width = cotangent.shape
    owner = tile_owner[:, 0]

    ring = ring_order(row_count)
    pos_of = np.argsort(np.array(ring))
    up = [(ring[p], ring[(p + 1) % row_count]) for p in range(row_count)]
    down = [(b, a) for a, b in up]
    far, near = row_count // 2, row_count - 1 - row_count // 2
    chains = [
        (0, 1, far),
        (0, -1, near),
        (1, 1, near),
        (1, -1, far),
    ]
    table = []
    for half, sign, hops in chains:
        for s in range(hops):
            table.append([ring[(pos_of[r] + sign * (hops - s)) % row_count] for r in range(row_count)])
    table.append(list(range(row_count)))
    table = jnp.asarray(np.array(table, dtype=np.int32).T)
    rows = lax.dynamic_index_in_dim(table, lax.axis_index("row"), 0, keepdims=False)

    grads = lax.all_gather(cotangent, "row", axis=0)

    step_hot = (
        step_ids[:, None] == jnp.arange(step_table.shape[0], dtype=jnp.int32)[None, :]
    ).astype(BF16)
    dims = (((0,), (1,)), ((), ()))
    pre_t = lax.dot_general(w_msg, node_feats, dims, preferred_element_type=F32)
    pre_t = pre_t + lax.dot_general(step_table, step_hot, dims, preferred_element_type=F32)
    msg_t = gelu_value(pre_t).astype(BF16)
    pre_t = lax.optimization_barrier(pre_t)
    nodes = msg_t.shape[1]
    msg = lax.all_to_all(
        msg_t.reshape(col_count, feats, nodes), "col", split_axis=0, concat_axis=0, tiled=True
    )

    held = [None] * len(chains)
    begun = []
    first = [sum(c[2] for c in chains[:i]) for i in range(len(chains))]
    for s in range(far):
        for i, (half, sign, hops) in enumerate(chains):
            skip = far - hops
            if s < skip:
                continue
            k = s - skip
            out = hop(
                first[i] + k, half, held[i], rows, owner, tile_dst_off, tile_src, msg, tile_vals, grads, width
            )
            if s == 0:
                begun.append(out)
            held[i] = lax.ppermute(out, "row", up if sign > 0 else down)
    which = sum(c[2] for c in chains)
    aggregated = last_hop(
        which, held, rows, owner, tile_dst_off, tile_src, msg, tile_vals, width
    )

    dmsg = back(owner, tile_dst_off, tile_src, grads, tile_vals, col_count, begun)
    return finish(node_feats, w_msg, pre_t, dmsg, aggregated)


def each_tile(meta, base, chip, body):
    def step(i, carry):
        body(i)
        return carry

    lax.fori_loop(meta[base + chip], meta[base + chip + 1], step, 0)


def sum_kernel(spec, ids, meta_own, meta_other, msg_own, msg_other, tiles_own, tiles_other, *refs):
    chips, picks, low, gates, split = spec
    recvs, rest = refs[: len(picks)], refs[len(picks) + gates :]
    outs, acc = rest[:-1], rest[-1]
    count, side, _ = tiles_own.shape
    feats = acc.shape[2]
    base = 4 * count
    total = None
    for ref, pick in zip(recvs, picks):
        part = ref[...] if pick is None else ref[pick : pick + 1]
        part = part.astype(F32).reshape(acc.shape)
        total = part if total is None else total + part
    acc[...] = jnp.zeros_like(acc) if total is None else total
    core = ids[ids.shape[0] - 1]
    for m, which in enumerate(chips):
        chip = ids[which]
        for meta, msg, tiles in ((meta_own, msg_own, tiles_own), (meta_other, msg_other, tiles_other)):
            per_part = msg.shape[2] // side

            def body(i, m=m, meta=meta, msg=msg, tiles=tiles, per_part=per_part):
                s = meta[2 * count + i]
                at = pl.ds(pl.multiple_of(lax.rem(s, per_part) * side, side), side)
                block = msg[lax.div(s, per_part), low : low + feats, at]
                part = lax.dot_general(
                    block,
                    tiles[meta[3 * count + i]],
                    (((1,), (1,)), ((), ())),
                    preferred_element_type=F32,
                )
                a = jnp.bitwise_xor(jnp.bitwise_and(meta[i], 1), core)
                to = pl.ds(pl.multiple_of(meta[count + i] * side, side), side)
                acc[m, a, :, to] = acc[m, a, :, to] + part

            each_tile(meta, base, chip, body)
    if split:
        for a in (0, 1):
            outs[a][...] = acc[0, a].astype(BF16)
    else:
        outs[0][...] = acc[...].astype(BF16).reshape(outs[0].shape)


def tile_sums(env, chips, recvs, low, feats, width, gates=(), split=False):
    ids, meta_own, meta_other, msg_own, msg_other, tiles_own, tiles_other = env
    smem = pl.BlockSpec(memory_space=pltpu.SMEM)
    vmem = pl.BlockSpec(memory_space=pltpu.VMEM)
    hbm = pl.BlockSpec(memory_space=pl.ANY)
    shape = (2, feats, width) if len(chips) == 1 else (len(chips), 2, feats, width)
    if split:
        out = [jax.ShapeDtypeStruct((feats, width), BF16)] * 2
    else:
        out = jax.ShapeDtypeStruct(shape, BF16)
    spec = (tuple(chips), tuple(p for _, p in recvs), low, len(gates), split)
    return pl.pallas_call(
        functools.partial(sum_kernel, spec),
        out_shape=out,
        in_specs=[smem] * 3 + [vmem] * (4 + len(recvs)) + [hbm] * len(gates),
        out_specs=[vmem] * 2 if split else vmem,
        scratch_shapes=[pltpu.VMEM((len(chips), 2, feats, width), F32)],
        compiler_params=pltpu.CompilerParams(vmem_limit_bytes=GRID_VMEM),
        cost_estimate=pl.CostEstimate(flops=2**28, bytes_accessed=4 * 2**20, transcendentals=0),
        name="tile_sums",
    )(ids, meta_own, meta_other, msg_own, msg_other, tiles_own, tiles_other, *[a for a, _ in recvs], *gates)


def grad_kernel(spec, ids, meta_own, meta_other, tiles_own, tiles_other, *refs):
    chips, has_sum, final = spec
    arrays, rest = refs[: len(chips)], refs[len(chips) :]
    count, side, _ = tiles_own.shape
    base = 4 * count
    if final:
        outs, acc = rest[-3:-1], rest[-1]
    else:
        acc = rest[-1]
    acc[...] = rest[0][...] if has_sum else jnp.zeros_like(acc)
    per_part = acc.shape[3] // side
    core = ids[ids.shape[0] - 1]
    for which, array in zip(chips, arrays):
        chip = ids[which]
        for q, (meta, tiles) in enumerate(((meta_own, tiles_own), (meta_other, tiles_other))):

            def body(i, q=q, meta=meta, tiles=tiles, array=array):
                a = jnp.bitwise_xor(jnp.bitwise_and(meta[i], 1), core)
                at = pl.ds(pl.multiple_of(meta[count + i] * side, side), side)
                term = jnp.dot(
                    array[a, :, at], tiles[meta[3 * count + i]], preferred_element_type=F32
                )
                s = meta[2 * count + i]
                part = lax.div(s, per_part)
                to = pl.ds(pl.multiple_of(lax.rem(s, per_part) * side, side), side)
                acc[q, part, :, to] = acc[q, part, :, to] + term

            each_tile(meta, base, chip, body)
    if final:
        for q in (0, 1):
            outs[q][...] = acc[q].astype(BF16)


def grad_sums(env, chips, arrays, so_far, parts, final):
    ids, meta_own, meta_other, _, _, tiles_own, tiles_other = env
    smem = pl.BlockSpec(memory_space=pltpu.SMEM)
    vmem = pl.BlockSpec(memory_space=pltpu.VMEM)
    _, feats, width = arrays[0].shape
    shape = (2, parts, feats, width // parts)
    if final:
        out = [jax.ShapeDtypeStruct(shape[1:], BF16)] * 2
        scratch = [pltpu.VMEM(shape, F32)]
    else:
        out = jax.ShapeDtypeStruct(shape, F32)
        scratch = []
    sums = [] if so_far is None else [so_far]
    return pl.pallas_call(
        functools.partial(grad_kernel, (tuple(chips), bool(sums), final)),
        out_shape=out,
        in_specs=[smem] * 3 + [vmem] * (2 + len(arrays) + len(sums)),
        out_specs=[vmem] * 2 if final else vmem,
        scratch_shapes=scratch,
        compiler_params=pltpu.CompilerParams(vmem_limit_bytes=GRID_VMEM),
        cost_estimate=pl.CostEstimate(flops=2**28, bytes_accessed=8 * 2**20, transcendentals=0),
        name="grad_sums",
    )(ids, meta_own, meta_other, tiles_own, tiles_other, *arrays, *sums)


def sorted_meta(owner, off, src, chips):
    count = owner.shape[0]
    key = owner // 2
    place = jnp.arange(count, dtype=jnp.int32)
    before = (key[None, :] < key[:, None]) | (
        (key[None, :] == key[:, None]) & (place[None, :] < place[:, None])
    )
    pos = jnp.sum(before.astype(jnp.int32), axis=1)
    hot = (pos[:, None] == place[None, :]).astype(jnp.int32)
    values = jnp.stack([owner, off, src, place])
    ordered = jnp.sum(values[:, :, None] * hot[None], axis=1)
    bounds = jnp.arange(chips + 2, dtype=jnp.int32)
    starts = jnp.sum((key[:, None] < bounds[None, :]).astype(jnp.int32), axis=0)
    return jnp.concatenate([ordered.reshape(-1), starts])


def grid_device(
    node_feats,
    w_msg,
    step_table,
    step_ids,
    tile_vals,
    tile_owner,
    tile_dst_off,
    tile_src,
    cotangent,
):
    row_count = lax.axis_size("row")
    col_count = lax.axis_size("col")
    feats, width = cotangent.shape
    slab = feats // 2
    feats_a = max(16, (5 * slab // 8) // 16 * 16)
    feats_b = slab - feats_a
    nz = row_count // 4
    chips = row_count // 2
    me = lax.axis_index("row")
    core = jnp.bitwise_and(me, 1)

    def z_of(r):
        return r // 4

    every = range(row_count)
    swap = [(r, r ^ 1) for r in every]

    def z_move(sign, ok):
        return [(r, r + 4 * sign) for r in every if 0 <= z_of(r) + sign < nz and ok(z_of(r))]

    def x_move(ok):
        return [(r, r ^ 2) for r in every if ok(z_of(r))]

    def rel(dz, dx):
        return (dz + nz - 1) * 2 + dx

    def turn(j, dx):
        return (2 * nz - 1) * 2 + j * 2 + dx

    table = np.zeros((row_count, (2 * nz - 1) * 2 + 2 * nz + 1), np.int32)
    for r in every:
        z, x, c = r // 4, (r // 2) % 2, r % 2
        for dx in (0, 1):
            for dz in range(1 - nz, nz):
                inside = 0 <= z + dz < nz
                table[r, rel(dz, dx)] = (z + dz) * 2 + (x ^ dx) if inside else chips
            for j in range(nz):
                table[r, turn(j, dx)] = ((z + j) % nz) * 2 + (x ^ dx)
        table[r, -1] = c
    ids = lax.dynamic_index_in_dim(jnp.asarray(table), me, 0, keepdims=False)

    def permute(a, pairs):
        return lax.ppermute(a, "row", pairs)

    def mine_and_other(a, axis):
        size = a.shape[axis] // 2
        mine = lax.dynamic_slice_in_dim(a, core * size, size, axis)
        other = lax.dynamic_slice_in_dim(a, (1 - core) * size, size, axis)
        return mine, other

    def in_order(mine, other, axis):
        first = jnp.where(core == 0, mine, other)
        second = jnp.where(core == 0, other, mine)
        return jnp.concatenate([first, second], axis=axis)

    mine, other = mine_and_other(cotangent, 0)
    partner = permute(other, swap)
    shard_a = jnp.stack([mine[:feats_a], partner[:feats_a]])
    shard_b = jnp.stack([mine[feats_a:], partner[feats_a:]])

    def z_line(array):
        got = {0: array}
        for k in range(1, nz):
            got[-k] = permute(got[1 - k], z_move(1, lambda z: z >= k - 1))
            got[k] = permute(got[k - 1], z_move(-1, lambda z: z + k - 1 < nz))
        return got

    across_b = permute(shard_b, x_move(lambda z: True))
    line_a = z_line(shard_a)
    line_b = z_line(shard_b)
    line_b2 = z_line(across_b)
    across_a = {
        dz: permute(line_a[dz], x_move(lambda z, dz=dz: 0 <= z + dz < nz)) for dz in line_a
    }

    meta_own = sorted_meta(tile_owner[:, 0], tile_dst_off, tile_src, chips)
    meta_other = permute(meta_own, swap)
    tiles_other = permute(tile_vals, swap)

    step_hot = (
        step_ids[:, None] == jnp.arange(step_table.shape[0], dtype=jnp.int32)[None, :]
    ).astype(BF16)
    dims = (((0,), (1,)), ((), ()))
    pre_t = lax.dot_general(w_msg, node_feats, dims, preferred_element_type=F32)
    pre_t = pre_t + lax.dot_general(step_table, step_hot, dims, preferred_element_type=F32)
    msg_t = gelu_value(pre_t).astype(BF16)
    pre_t = lax.optimization_barrier(pre_t)
    nodes = msg_t.shape[1]
    msg = lax.all_to_all(
        msg_t.reshape(col_count, feats, nodes), "col", split_axis=0, concat_axis=0, tiled=True
    )
    msg_own, other = mine_and_other(msg, 1)
    msg_other = permute(other, swap)
    env = (ids, meta_own, meta_other, msg_own, msg_other, tile_vals, tiles_other)

    def sums_a(chip, recvs, split=False):
        return tile_sums(env, [chip], recvs, 0, feats_a, width, split=split)

    def sums_b(picks, recvs, split=False):
        return tile_sums(env, picks, recvs, feats_a, feats_b, width, split=split)

    from_x = {
        j: permute(sums_a(turn(j, 1), []), x_move(lambda z: True))
        for j in sorted(range(nz), key=lambda j: -min(j, nz - j))
    }
    up_a = down_a = up_b = down_b = None
    for d in range(nz - 1, 0, -1):
        more = [] if up_b is None else [(up_b, None)]
        up_b = permute(sums_b([rel(d, 0), rel(d, 1)], more), z_move(1, lambda z: z + d < nz))
        more = [] if down_b is None else [(down_b, None)]
        down_b = permute(sums_b([rel(-d, 0), rel(-d, 1)], more), z_move(-1, lambda z: z >= d))
    for d in range(nz - 1, 0, -1):
        more = [(from_x[d], None)] + ([] if up_a is None else [(up_a, None)])
        up_a = permute(sums_a(rel(d, 0), more), z_move(1, lambda z: z + d < nz))
        more = [(from_x[nz - d], None)] + ([] if down_a is None else [(down_a, None)])
        down_a = permute(sums_a(rel(-d, 0), more), z_move(-1, lambda z: z >= d))
    recv_b = permute(
        sums_b([rel(0, 1)], [(up_b, 1), (down_b, 1)]), x_move(lambda z: True)
    )
    keep_b, send_b = sums_b([rel(0, 0)], [(up_b, 0), (down_b, 0), (recv_b, None)], split=True)
    keep_a, send_a = sums_a(
        rel(0, 0), [(from_x[0], None), (up_a, None), (down_a, None)], split=True
    )
    other_a, other_b = permute(send_a, swap), permute(send_b, swap)
    aggregated = in_order(
        jnp.concatenate([keep_a, keep_b]), jnp.concatenate([other_a, other_b]), 0
    )

    def near(dz):
        return abs(dz) <= 1

    def grads(pairs, so_far, final):
        return grad_sums(env, [w for w, _ in pairs], [a for _, a in pairs], so_far, col_count, final)

    acc_a = grads([(rel(dz, 0), a) for dz, a in line_a.items()], None, False)
    acc_b = grads(
        [(rel(dz, 0), a) for dz, a in line_b.items() if near(dz)]
        + [(rel(dz, 1), a) for dz, a in line_b2.items() if near(dz)],
        None,
        False,
    )
    own_a, send_a = grads([(rel(dz, 1), a) for dz, a in across_a.items()], acc_a, True)
    own_b, send_b = grads(
        [(rel(dz, 0), a) for dz, a in line_b.items() if not near(dz)]
        + [(rel(dz, 1), a) for dz, a in line_b2.items() if not near(dz)],
        acc_b,
        True,
    )
    other_a, other_b = permute(send_a, swap), permute(send_b, swap)
    dmsg = in_order(
        jnp.concatenate([own_a, own_b], axis=1), jnp.concatenate([other_a, other_b], axis=1), 1
    )
    return finish(node_feats, w_msg, pre_t, dmsg, aggregated)


def finish(node_feats, w_msg, pre_t, dmsg, aggregated):
    dims = (((0,), (1,)), ((), ()))
    dmsg_rows = lax.all_to_all(dmsg, "col", split_axis=0, concat_axis=0, tiled=True)
    dmsg_rows = dmsg_rows.reshape(pre_t.shape)
    dpre_t = (dmsg_rows.astype(F32) * gelu_slope(pre_t)).astype(BF16)
    feat_grad = lax.dot_general(dpre_t, w_msg, dims, preferred_element_type=F32).astype(BF16)
    weight_term = lax.dot_general(
        node_feats, dpre_t, dims, preferred_element_type=F32
    ).astype(BF16)
    devices = lax.axis_size("row") * lax.axis_size("col")
    hidden = weight_term.shape[0]
    shares = lax.all_to_all(
        weight_term.reshape(devices, hidden // devices, hidden),
        ("row", "col"),
        split_axis=0,
        concat_axis=0,
        tiled=True,
    )
    share = jnp.sum(shares.astype(F32), axis=0).astype(BF16)
    weight_grad = lax.all_to_all(
        jnp.broadcast_to(share[None], (devices,) + share.shape),
        ("row", "col"),
        split_axis=0,
        concat_axis=0,
        tiled=True,
    ).reshape(hidden, hidden)
    return (aggregated, feat_grad, weight_grad)


def solution(mesh):
    rows = mesh.shape["row"]
    chips = rows // 2
    per_device = grid_device if rows % 4 == 0 and chips <= 8 else ring_device
    return jax.shard_map(
        per_device,
        mesh=mesh,
        in_specs=(
            P(("row", "col"), None),
            P(),
            P(),
            P(("row", "col")),
            P("row", None, None),
            P("row", None),
            P("row"),
            P("row"),
            P("col", "row"),
        ),
        out_specs=(P("col", "row"), P(("row", "col"), None), P()),
        check_vma=False,
    )
```

```python
import functools

import jax
import jax.numpy as jnp
import numpy as np
from jax import lax
from jax.experimental import pallas as pl
from jax.experimental.pallas import tpu as pltpu
from jax.sharding import PartitionSpec as P


F32 = jnp.float32
BF16 = jnp.bfloat16
VMEM_LIMIT = 48 * 1024 * 1024
GRID_VMEM = 40 * 1024 * 1024


def gelu_value(v):
    return 0.5 * v * (1.0 + jax.scipy.special.erf(v / jnp.sqrt(2.0)))


def gelu_slope(v):
    return 0.5 * (1.0 + jax.scipy.special.erf(v / jnp.sqrt(2.0))) + v * jnp.exp(
        -0.5 * v * v
    ) / jnp.sqrt(2.0 * jnp.pi)


def ring_order(row_count):
    chips = row_count // 2
    bits = max(chips.bit_length() - 1, 0)
    nz = 1 << ((bits + 1) // 2)
    nx = chips // nz
    path = []
    for x in range(nx):
        zs = range(1, nz) if x % 2 == 0 else range(nz - 1, 0, -1)
        if nz == 1:
            zs = range(0)
        path += [(z, x) for z in zs]
    path += [(0, x) for x in range(nx - 1, -1, -1)]
    order = []
    for z, x in path:
        order += [(z * nx + x) * 2, (z * nx + x) * 2 + 1]
    return order


def add_tiles(acc_ref, row, owner, off, src, msg_ref, tiles_ref, side):
    per_part = msg_ref.shape[2] // side

    def step(t, carry):
        @pl.when(owner[t] == row)
        def _():
            s = src[t]
            col = pl.multiple_of(lax.rem(s, per_part) * side, side)
            feats = msg_ref[lax.div(s, per_part), :, pl.ds(col, side)]
            part = lax.dot_general(
                feats, tiles_ref[t], (((1,), (1,)), ((), ())), preferred_element_type=F32
            )
            at = pl.ds(pl.multiple_of(off[t] * side, side), side)
            acc_ref[:, at] = acc_ref[:, at] + part

        return carry

    lax.fori_loop(0, tiles_ref.shape[0], step, 0)


def hop_kernel(which, has_recv, side, rows, owner, off, src, *refs):
    if has_recv:
        recv_ref, msg_ref, tiles_ref, _, out_ref, acc_ref = refs
        acc_ref[...] = recv_ref[...].astype(F32)
    else:
        msg_ref, tiles_ref, _, out_ref, acc_ref = refs
        acc_ref[...] = jnp.zeros_like(acc_ref)
    add_tiles(acc_ref, rows[which], owner, off, src, msg_ref, tiles_ref, side)
    out_ref[...] = acc_ref[...].astype(out_ref.dtype)


def hop(which, half, recv, rows, owner, off, src, msg, tiles, gate, width):
    parts, feats, part_nodes = msg.shape
    fh = feats // 2
    side = tiles.shape[1]
    args = ([recv] if recv is not None else []) + [msg, tiles, gate]
    vm = pl.BlockSpec(memory_space=pltpu.VMEM)
    full = pl.BlockSpec((fh, width), lambda i, *_: (0, 0))
    specs = ([full] if recv is not None else []) + [
        pl.BlockSpec((parts, fh, part_nodes), lambda i, *_: (0, half, 0)),
        pl.BlockSpec(tiles.shape, lambda i, *_: (0, 0, 0)),
        pl.BlockSpec(memory_space=pl.ANY),
    ]
    return pl.pallas_call(
        functools.partial(hop_kernel, which, recv is not None, side),
        out_shape=jax.ShapeDtypeStruct((fh, width), BF16),
        grid_spec=pltpu.PrefetchScalarGridSpec(
            num_scalar_prefetch=4,
            grid=(1,),
            in_specs=specs,
            out_specs=full,
            scratch_shapes=[pltpu.VMEM((fh, width), F32)],
        ),
        compiler_params=pltpu.CompilerParams(vmem_limit_bytes=VMEM_LIMIT),
        cost_estimate=pl.CostEstimate(
            flops=2 * fh * side * side * 9, bytes_accessed=6 * 2**20, transcendentals=0
        ),
        name="hop",
    )(rows, owner, off, src, *args)


def last_kernel(which, side, rows, owner, off, src, p0, m0, p1, m1, msg_ref, tiles_ref, out_ref, acc_ref):
    fh = p0.shape[0]
    acc_ref[:fh, :] = p0[...].astype(F32) + m0[...].astype(F32)
    acc_ref[fh:, :] = p1[...].astype(F32) + m1[...].astype(F32)
    add_tiles(acc_ref, rows[which], owner, off, src, msg_ref, tiles_ref, side)
    out_ref[...] = acc_ref[...].astype(out_ref.dtype)


def last_hop(which, recvs, rows, owner, off, src, msg, tiles, width):
    _, feats, _ = msg.shape
    side = tiles.shape[1]
    half = pl.BlockSpec((feats // 2, width), lambda i, *_: (0, 0))
    return pl.pallas_call(
        functools.partial(last_kernel, which, side),
        out_shape=jax.ShapeDtypeStruct((feats, width), BF16),
        grid_spec=pltpu.PrefetchScalarGridSpec(
            num_scalar_prefetch=4,
            grid=(1,),
            in_specs=[half] * 4
            + [
                pl.BlockSpec(msg.shape, lambda i, *_: (0, 0, 0)),
                pl.BlockSpec(tiles.shape, lambda i, *_: (0, 0, 0)),
            ],
            out_specs=pl.BlockSpec((feats, width), lambda i, *_: (0, 0)),
            scratch_shapes=[pltpu.VMEM((feats, width), F32)],
        ),
        compiler_params=pltpu.CompilerParams(vmem_limit_bytes=VMEM_LIMIT),
        name="last_hop",
    )(rows, owner, off, src, *recvs, msg, tiles)


def back_kernel(side, owner, off, src, grads_ref, tiles_ref, *refs):
    out_ref, buf_ref, acc_ref, sem = refs[-4:]
    count = tiles_ref.shape[0]
    per_part = out_ref.shape[2] // side

    def fetch(t):
        at = pl.ds(pl.multiple_of(off[t] * side, side), side)
        return pltpu.make_async_copy(grads_ref.at[owner[t], :, at], buf_ref.at[t], sem.at[t])

    def begin(t, carry):
        fetch(t).start()
        return carry

    lax.fori_loop(0, count, begin, 0)
    acc_ref[...] = jnp.zeros_like(acc_ref)

    def step(t, carry):
        fetch(t).wait()
        term = jnp.dot(buf_ref[t], tiles_ref[t], preferred_element_type=F32)
        s = src[t]
        at = pl.ds(pl.multiple_of(lax.rem(s, per_part) * side, side), side)
        part = lax.div(s, per_part)
        acc_ref[part, :, at] = acc_ref[part, :, at] + term
        return carry

    lax.fori_loop(0, count, step, 0)
    out_ref[...] = acc_ref[...].astype(out_ref.dtype)


def back(owner, off, src, grads, tiles, parts, after):
    _, feats, width = grads.shape
    count, side, _ = tiles.shape
    shape = (parts, feats, width // parts)
    return pl.pallas_call(
        functools.partial(back_kernel, side),
        out_shape=jax.ShapeDtypeStruct(shape, BF16),
        grid_spec=pltpu.PrefetchScalarGridSpec(
            num_scalar_prefetch=3,
            grid=(1,),
            in_specs=[
                pl.BlockSpec(memory_space=pl.ANY),
                pl.BlockSpec(tiles.shape, lambda i, *_: (0, 0, 0)),
            ]
            + [pl.BlockSpec(memory_space=pl.ANY)] * len(after),
            out_specs=pl.BlockSpec(shape, lambda i, *_: (0, 0, 0)),
            scratch_shapes=[
                pltpu.VMEM((count, feats, side), BF16),
                pltpu.VMEM(shape, F32),
                pltpu.SemaphoreType.DMA((count,)),
            ],
        ),
        compiler_params=pltpu.CompilerParams(vmem_limit_bytes=VMEM_LIMIT),
        cost_estimate=pl.CostEstimate(
            flops=2 * feats * side * side * count, bytes_accessed=30 * 2**20, transcendentals=0
        ),
        name="back",
    )(owner, off, src, grads, tiles, *after)


def ring_device(
    node_feats,
    w_msg,
    step_table,
    step_ids,
    tile_vals,
    tile_owner,
    tile_dst_off,
    tile_src,
    cotangent,
):
    row_count = lax.axis_size("row")
    col_count = lax.axis_size("col")
    feats, width = cotangent.shape
    owner = tile_owner[:, 0]

    ring = ring_order(row_count)
    pos_of = np.argsort(np.array(ring))
    up = [(ring[p], ring[(p + 1) % row_count]) for p in range(row_count)]
    down = [(b, a) for a, b in up]
    far, near = row_count // 2, row_count - 1 - row_count // 2
    chains = [
        (0, 1, far),
        (0, -1, near),
        (1, 1, near),
        (1, -1, far),
    ]
    table = []
    for half, sign, hops in chains:
        for s in range(hops):
            table.append([ring[(pos_of[r] + sign * (hops - s)) % row_count] for r in range(row_count)])
    table.append(list(range(row_count)))
    table = jnp.asarray(np.array(table, dtype=np.int32).T)
    rows = lax.dynamic_index_in_dim(table, lax.axis_index("row"), 0, keepdims=False)

    grads = lax.all_gather(cotangent, "row", axis=0)

    step_hot = (
        step_ids[:, None] == jnp.arange(step_table.shape[0], dtype=jnp.int32)[None, :]
    ).astype(BF16)
    dims = (((0,), (1,)), ((), ()))
    pre_t = lax.dot_general(w_msg, node_feats, dims, preferred_element_type=F32)
    pre_t = pre_t + lax.dot_general(step_table, step_hot, dims, preferred_element_type=F32)
    msg_t = gelu_value(pre_t).astype(BF16)
    pre_t = lax.optimization_barrier(pre_t)
    nodes = msg_t.shape[1]
    msg = lax.all_to_all(
        msg_t.reshape(col_count, feats, nodes), "col", split_axis=0, concat_axis=0, tiled=True
    )

    held = [None] * len(chains)
    begun = []
    first = [sum(c[2] for c in chains[:i]) for i in range(len(chains))]
    for s in range(far):
        for i, (half, sign, hops) in enumerate(chains):
            skip = far - hops
            if s < skip:
                continue
            k = s - skip
            out = hop(
                first[i] + k, half, held[i], rows, owner, tile_dst_off, tile_src, msg, tile_vals, grads, width
            )
            if s == 0:
                begun.append(out)
            held[i] = lax.ppermute(out, "row", up if sign > 0 else down)
    which = sum(c[2] for c in chains)
    aggregated = last_hop(
        which, held, rows, owner, tile_dst_off, tile_src, msg, tile_vals, width
    )

    dmsg = back(owner, tile_dst_off, tile_src, grads, tile_vals, col_count, begun)
    return finish(node_feats, w_msg, pre_t, dmsg, aggregated)


GROUP = 4


def each_tile(meta, base, chip, product, add):
    low, high = meta[base + chip], meta[base + chip + 1]

    def step(g, carry):
        at = [low + g * GROUP + u for u in range(GROUP)]
        use = [jnp.minimum(i, high - 1) for i in at]
        parts = [product(i) for i in use]
        for i, j, part in zip(at, use, parts):
            add(j, jnp.where(i < high, part, 0.0))
        return carry

    lax.fori_loop(0, lax.div(high - low + GROUP - 1, GROUP), step, 0)


def sum_kernel(spec, ids, meta_own, meta_other, msg_own, msg_other, tiles_own, tiles_other, *refs):
    chips, picks, low, gates, split = spec
    recvs, rest = refs[: len(picks)], refs[len(picks) + gates :]
    outs, acc = rest[:-1], rest[-1]
    count, side, _ = tiles_own.shape
    feats = acc.shape[2]
    base = 4 * count
    total = None
    for ref, pick in zip(recvs, picks):
        part = ref[...] if pick is None else ref[pick : pick + 1]
        part = part.astype(F32).reshape(acc.shape)
        total = part if total is None else total + part
    acc[...] = jnp.zeros_like(acc) if total is None else total
    core = ids[ids.shape[0] - 1]
    for m, which in enumerate(chips):
        chip = ids[which]
        for meta, msg, tiles in ((meta_own, msg_own, tiles_own), (meta_other, msg_other, tiles_other)):
            per_part = msg.shape[2] // side

            def product(i, meta=meta, msg=msg, tiles=tiles, per_part=per_part):
                s = meta[2 * count + i]
                at = pl.ds(pl.multiple_of(lax.rem(s, per_part) * side, side), side)
                block = msg[lax.div(s, per_part), low : low + feats, at]
                return lax.dot_general(
                    block,
                    tiles[meta[3 * count + i]],
                    (((1,), (1,)), ((), ())),
                    preferred_element_type=F32,
                )

            def add(i, part, m=m, meta=meta):
                a = jnp.bitwise_xor(jnp.bitwise_and(meta[i], 1), core)
                to = pl.ds(pl.multiple_of(meta[count + i] * side, side), side)
                acc[m, a, :, to] = acc[m, a, :, to] + part

            each_tile(meta, base, chip, product, add)
    if split:
        for a in (0, 1):
            outs[a][...] = acc[0, a].astype(BF16)
    else:
        outs[0][...] = acc[...].astype(BF16).reshape(outs[0].shape)


def tile_sums(env, chips, recvs, low, feats, width, gates=(), split=False):
    ids, meta_own, meta_other, msg_own, msg_other, tiles_own, tiles_other = env
    smem = pl.BlockSpec(memory_space=pltpu.SMEM)
    vmem = pl.BlockSpec(memory_space=pltpu.VMEM)
    hbm = pl.BlockSpec(memory_space=pl.ANY)
    shape = (2, feats, width) if len(chips) == 1 else (len(chips), 2, feats, width)
    if split:
        out = [jax.ShapeDtypeStruct((feats, width), BF16)] * 2
    else:
        out = jax.ShapeDtypeStruct(shape, BF16)
    spec = (tuple(chips), tuple(p for _, p in recvs), low, len(gates), split)
    return pl.pallas_call(
        functools.partial(sum_kernel, spec),
        out_shape=out,
        in_specs=[smem] * 3 + [vmem] * (4 + len(recvs)) + [hbm] * len(gates),
        out_specs=[vmem] * 2 if split else vmem,
        scratch_shapes=[pltpu.VMEM((len(chips), 2, feats, width), F32)],
        compiler_params=pltpu.CompilerParams(vmem_limit_bytes=GRID_VMEM),
        cost_estimate=pl.CostEstimate(flops=2**28, bytes_accessed=4 * 2**20, transcendentals=0),
        name="tile_sums",
    )(ids, meta_own, meta_other, msg_own, msg_other, tiles_own, tiles_other, *[a for a, _ in recvs], *gates)


def grad_kernel(spec, ids, meta_own, meta_other, tiles_own, tiles_other, *refs):
    chips, has_sum, final = spec
    arrays, rest = refs[: len(chips)], refs[len(chips) :]
    count, side, _ = tiles_own.shape
    base = 4 * count
    if final:
        outs, acc = rest[-3:-1], rest[-1]
    else:
        acc = rest[-1]
    acc[...] = rest[0][...] if has_sum else jnp.zeros_like(acc)
    per_part = acc.shape[3] // side
    core = ids[ids.shape[0] - 1]
    for which, array in zip(chips, arrays):
        chip = ids[which]
        for q, (meta, tiles) in enumerate(((meta_own, tiles_own), (meta_other, tiles_other))):

            def product(i, meta=meta, tiles=tiles, array=array):
                a = jnp.bitwise_xor(jnp.bitwise_and(meta[i], 1), core)
                at = pl.ds(pl.multiple_of(meta[count + i] * side, side), side)
                return jnp.dot(
                    array[a, :, at], tiles[meta[3 * count + i]], preferred_element_type=F32
                )

            def add(i, term, q=q, meta=meta):
                s = meta[2 * count + i]
                part = lax.div(s, per_part)
                to = pl.ds(pl.multiple_of(lax.rem(s, per_part) * side, side), side)
                acc[q, part, :, to] = acc[q, part, :, to] + term

            each_tile(meta, base, chip, product, add)
    if final:
        for q in (0, 1):
            outs[q][...] = acc[q].astype(BF16)


def grad_sums(env, chips, arrays, so_far, parts, final):
    ids, meta_own, meta_other, _, _, tiles_own, tiles_other = env
    smem = pl.BlockSpec(memory_space=pltpu.SMEM)
    vmem = pl.BlockSpec(memory_space=pltpu.VMEM)
    _, feats, width = arrays[0].shape
    shape = (2, parts, feats, width // parts)
    if final:
        out = [jax.ShapeDtypeStruct(shape[1:], BF16)] * 2
        scratch = [pltpu.VMEM(shape, F32)]
    else:
        out = jax.ShapeDtypeStruct(shape, F32)
        scratch = []
    sums = [] if so_far is None else [so_far]
    return pl.pallas_call(
        functools.partial(grad_kernel, (tuple(chips), bool(sums), final)),
        out_shape=out,
        in_specs=[smem] * 3 + [vmem] * (2 + len(arrays) + len(sums)),
        out_specs=[vmem] * 2 if final else vmem,
        scratch_shapes=scratch,
        compiler_params=pltpu.CompilerParams(vmem_limit_bytes=GRID_VMEM),
        cost_estimate=pl.CostEstimate(flops=2**28, bytes_accessed=8 * 2**20, transcendentals=0),
        name="grad_sums",
    )(ids, meta_own, meta_other, tiles_own, tiles_other, *arrays, *sums)


def sorted_meta(owner, off, src, chips):
    count = owner.shape[0]
    key = owner // 2
    place = jnp.arange(count, dtype=jnp.int32)
    before = (key[None, :] < key[:, None]) | (
        (key[None, :] == key[:, None]) & (place[None, :] < place[:, None])
    )
    pos = jnp.sum(before.astype(jnp.int32), axis=1)
    hot = (pos[:, None] == place[None, :]).astype(jnp.int32)
    values = jnp.stack([owner, off, src, place])
    ordered = jnp.sum(values[:, :, None] * hot[None], axis=1)
    bounds = jnp.arange(chips + 2, dtype=jnp.int32)
    starts = jnp.sum((key[:, None] < bounds[None, :]).astype(jnp.int32), axis=0)
    return jnp.concatenate([ordered.reshape(-1), starts])


def grid_device(
    node_feats,
    w_msg,
    step_table,
    step_ids,
    tile_vals,
    tile_owner,
    tile_dst_off,
    tile_src,
    cotangent,
):
    row_count = lax.axis_size("row")
    col_count = lax.axis_size("col")
    feats, width = cotangent.shape
    slab = feats // 2
    feats_a = max(16, (3 * slab // 8) // 16 * 16)
    feats_b = slab - feats_a
    nz = row_count // 4
    chips = row_count // 2
    me = lax.axis_index("row")
    core = jnp.bitwise_and(me, 1)
    every = range(row_count)
    swap = [(r, r ^ 1) for r in every]

    def z_move(sign, ok):
        return [(r, r + 4 * sign) for r in every if 0 <= r // 4 + sign < nz and ok(r // 4)]

    def x_move(ok):
        return [(r, r ^ 2) for r in every if ok(r // 4)]

    def rel(dz, dx):
        return (dz + nz - 1) * 2 + dx

    def turn(j, dx):
        return (2 * nz - 1) * 2 + j * 2 + dx

    table = np.zeros((row_count, (2 * nz - 1) * 2 + 2 * nz + 1), np.int32)
    for r in every:
        z, x, c = r // 4, (r // 2) % 2, r % 2
        for dx in (0, 1):
            for dz in range(1 - nz, nz):
                inside = 0 <= z + dz < nz
                table[r, rel(dz, dx)] = (z + dz) * 2 + (x ^ dx) if inside else chips
            for j in range(nz):
                table[r, turn(j, dx)] = ((z + j) % nz) * 2 + (x ^ dx)
        table[r, -1] = c
    ids = lax.dynamic_index_in_dim(jnp.asarray(table), me, 0, keepdims=False)

    def permute(a, pairs):
        return lax.ppermute(a, "row", pairs)

    def mine_and_other(a, axis):
        size = a.shape[axis] // 2
        mine = lax.dynamic_slice_in_dim(a, core * size, size, axis)
        other = lax.dynamic_slice_in_dim(a, (1 - core) * size, size, axis)
        return mine, other

    def in_order(mine, other, axis):
        first = jnp.where(core == 0, mine, other)
        second = jnp.where(core == 0, other, mine)
        return jnp.concatenate([first, second], axis=axis)

    mine, other = mine_and_other(cotangent, 0)
    shard = jnp.stack([mine, permute(other, swap)])
    line = {0: shard}
    across = {0: permute(shard, x_move(lambda z: True))}
    for k in range(1, nz):
        for sign in (-1, 1):
            pairs = z_move(-sign, lambda z: 0 <= z + sign * (k - 1) < nz)
            line[sign * k] = permute(line[sign * (k - 1)], pairs)
        for sign in (-1, 1):
            pairs = x_move(lambda z: 0 <= z + sign * k < nz)
            across[sign * k] = permute(line[sign * k], pairs)

    meta_own = sorted_meta(tile_owner[:, 0], tile_dst_off, tile_src, chips)
    meta_other = permute(meta_own, swap)
    tiles_other = permute(tile_vals, swap)

    step_hot = (
        step_ids[:, None] == jnp.arange(step_table.shape[0], dtype=jnp.int32)[None, :]
    ).astype(BF16)
    dims = (((0,), (1,)), ((), ()))
    pre_t = lax.dot_general(w_msg, node_feats, dims, preferred_element_type=F32)
    pre_t = pre_t + lax.dot_general(step_table, step_hot, dims, preferred_element_type=F32)
    msg_t = gelu_value(pre_t).astype(BF16)
    pre_t = lax.optimization_barrier(pre_t)
    nodes = msg_t.shape[1]
    msg = lax.all_to_all(
        msg_t.reshape(col_count, feats, nodes), "col", split_axis=0, concat_axis=0, tiled=True
    )
    msg_own, other = mine_and_other(msg, 1)
    msg_other = permute(other, swap)
    env = (ids, meta_own, meta_other, msg_own, msg_other, tile_vals, tiles_other)

    def sums_a(chip, recvs, split=False):
        return tile_sums(env, [chip], recvs, 0, feats_a, width, split=split)

    def sums_b(picks, recvs, split=False):
        return tile_sums(env, picks, recvs, feats_a, feats_b, width, split=split)

    def known(a):
        return [] if a is None else [(a, None)]

    from_x = {j: permute(sums_a(turn(j, 1), []), x_move(lambda z: True)) for j in range(nz)}
    flow_a, flow_b = {-1: None, 1: None}, {-1: None, 1: None}
    for d in range(nz - 1, 0, -1):
        for sign in (1, -1):
            pairs = z_move(sign, lambda z: 0 <= z + sign * d < nz)
            out = sums_b([rel(sign * d, 0), rel(sign * d, 1)], known(flow_b[sign]))
            flow_b[sign] = permute(out, pairs)
            out = sums_a(rel(sign * d, 0), known(from_x[sign * d % nz]) + known(flow_a[sign]))
            flow_a[sign] = permute(out, pairs)
    recv_b = permute(sums_b([rel(0, 1)], [(flow_b[1], 1), (flow_b[-1], 1)]), x_move(lambda z: True))
    keep_b, send_b = sums_b(
        [rel(0, 0)], [(flow_b[1], 0), (flow_b[-1], 0), (recv_b, None)], split=True
    )
    keep_a, send_a = sums_a(
        rel(0, 0), known(from_x[0]) + known(flow_a[1]) + known(flow_a[-1]), split=True
    )
    other_a, other_b = permute(send_a, swap), permute(send_b, swap)
    aggregated = in_order(
        jnp.concatenate([keep_a, keep_b]), jnp.concatenate([other_a, other_b]), 0
    )

    def grads(dx, steps, so_far, final=False):
        arrays = [(line, across)[dx][dz] for dz in steps]
        return grad_sums(env, [rel(dz, dx) for dz in steps], arrays, so_far, col_count, final)

    near = [dz for dz in line if abs(dz) <= 1]
    far = [dz for dz in line if abs(dz) > 1]
    acc = grads(0, near, None)
    acc = grads(0, far, acc)
    acc = grads(1, near, acc)
    own, send = grads(1, far, acc, True)
    dmsg = in_order(own, permute(send, swap), 1)
    return finish(node_feats, w_msg, pre_t, dmsg, aggregated)


def finish(node_feats, w_msg, pre_t, dmsg, aggregated):
    dims = (((0,), (1,)), ((), ()))
    dmsg_rows = lax.all_to_all(dmsg, "col", split_axis=0, concat_axis=0, tiled=True)
    dmsg_rows = dmsg_rows.reshape(pre_t.shape)
    dpre_t = (dmsg_rows.astype(F32) * gelu_slope(pre_t)).astype(BF16)
    feat_grad = lax.dot_general(dpre_t, w_msg, dims, preferred_element_type=F32).astype(BF16)
    weight_term = lax.dot_general(
        node_feats, dpre_t, dims, preferred_element_type=F32
    ).astype(BF16)
    devices = lax.axis_size("row") * lax.axis_size("col")
    hidden = weight_term.shape[0]
    rows_each = hidden // devices
    axes = ("row", "col")
    shares = lax.all_to_all(
        weight_term.reshape(devices, rows_each, hidden), axes, split_axis=0, concat_axis=0, tiled=True
    )
    share = jnp.sum(shares.astype(F32), axis=0).astype(BF16)
    weight_grad = lax.all_to_all(
        jnp.broadcast_to(share[None], (devices,) + share.shape), axes, split_axis=0, concat_axis=0, tiled=True
    ).reshape(hidden, hidden)
    return (aggregated, feat_grad, weight_grad)


def solution(mesh):
    rows = mesh.shape["row"]
    in_grid = rows == 16

    def per_device(*args):
        return (grid_device if in_grid else ring_device)(*args)

    return jax.shard_map(
        per_device,
        mesh=mesh,
        in_specs=(
            P(("row", "col"), None),
            P(),
            P(),
            P(("row", "col")),
            P("row", None, None),
            P("row", None),
            P("row"),
            P("row"),
            P("col", "row"),
        ),
        out_specs=(P("col", "row"), P(("row", "col"), None), P()),
        check_vma=False,
    )
```

```python
import functools

import jax
import jax.numpy as jnp
import numpy as np
from jax import lax
from jax.experimental import pallas as pl
from jax.experimental.pallas import tpu as pltpu
from jax.sharding import PartitionSpec as P


F32 = jnp.float32
BF16 = jnp.bfloat16
VMEM_LIMIT = 48 * 1024 * 1024
GRID_VMEM = 32 * 1024 * 1024
PARTS_VMEM = 20 * 1024 * 1024
SMALL_VMEM = 16 * 1024 * 1024


def gelu_value(v):
    return 0.5 * v * (1.0 + jax.scipy.special.erf(v / jnp.sqrt(2.0)))


def gelu_slope(v):
    return 0.5 * (1.0 + jax.scipy.special.erf(v / jnp.sqrt(2.0))) + v * jnp.exp(
        -0.5 * v * v
    ) / jnp.sqrt(2.0 * jnp.pi)


def ring_order(row_count):
    chips = row_count // 2
    bits = max(chips.bit_length() - 1, 0)
    nz = 1 << ((bits + 1) // 2)
    nx = chips // nz
    path = []
    for x in range(nx):
        zs = range(1, nz) if x % 2 == 0 else range(nz - 1, 0, -1)
        if nz == 1:
            zs = range(0)
        path += [(z, x) for z in zs]
    path += [(0, x) for x in range(nx - 1, -1, -1)]
    order = []
    for z, x in path:
        order += [(z * nx + x) * 2, (z * nx + x) * 2 + 1]
    return order


def add_tiles(acc_ref, row, owner, off, src, msg_ref, tiles_ref, side):
    per_part = msg_ref.shape[2] // side

    def step(t, carry):
        @pl.when(owner[t] == row)
        def _():
            s = src[t]
            col = pl.multiple_of(lax.rem(s, per_part) * side, side)
            feats = msg_ref[lax.div(s, per_part), :, pl.ds(col, side)]
            part = lax.dot_general(
                feats, tiles_ref[t], (((1,), (1,)), ((), ())), preferred_element_type=F32
            )
            at = pl.ds(pl.multiple_of(off[t] * side, side), side)
            acc_ref[:, at] = acc_ref[:, at] + part

        return carry

    lax.fori_loop(0, tiles_ref.shape[0], step, 0)


def hop_kernel(which, has_recv, side, rows, owner, off, src, *refs):
    if has_recv:
        recv_ref, msg_ref, tiles_ref, _, out_ref, acc_ref = refs
        acc_ref[...] = recv_ref[...].astype(F32)
    else:
        msg_ref, tiles_ref, _, out_ref, acc_ref = refs
        acc_ref[...] = jnp.zeros_like(acc_ref)
    add_tiles(acc_ref, rows[which], owner, off, src, msg_ref, tiles_ref, side)
    out_ref[...] = acc_ref[...].astype(out_ref.dtype)


def hop(which, half, recv, rows, owner, off, src, msg, tiles, gate, width):
    parts, feats, part_nodes = msg.shape
    fh = feats // 2
    side = tiles.shape[1]
    args = ([recv] if recv is not None else []) + [msg, tiles, gate]
    vm = pl.BlockSpec(memory_space=pltpu.VMEM)
    full = pl.BlockSpec((fh, width), lambda i, *_: (0, 0))
    specs = ([full] if recv is not None else []) + [
        pl.BlockSpec((parts, fh, part_nodes), lambda i, *_: (0, half, 0)),
        pl.BlockSpec(tiles.shape, lambda i, *_: (0, 0, 0)),
        pl.BlockSpec(memory_space=pl.ANY),
    ]
    return pl.pallas_call(
        functools.partial(hop_kernel, which, recv is not None, side),
        out_shape=jax.ShapeDtypeStruct((fh, width), BF16),
        grid_spec=pltpu.PrefetchScalarGridSpec(
            num_scalar_prefetch=4,
            grid=(1,),
            in_specs=specs,
            out_specs=full,
            scratch_shapes=[pltpu.VMEM((fh, width), F32)],
        ),
        compiler_params=pltpu.CompilerParams(vmem_limit_bytes=VMEM_LIMIT),
        cost_estimate=pl.CostEstimate(
            flops=2 * fh * side * side * 9, bytes_accessed=6 * 2**20, transcendentals=0
        ),
        name="hop",
    )(rows, owner, off, src, *args)


def last_kernel(which, side, rows, owner, off, src, p0, m0, p1, m1, msg_ref, tiles_ref, out_ref, acc_ref):
    fh = p0.shape[0]
    acc_ref[:fh, :] = p0[...].astype(F32) + m0[...].astype(F32)
    acc_ref[fh:, :] = p1[...].astype(F32) + m1[...].astype(F32)
    add_tiles(acc_ref, rows[which], owner, off, src, msg_ref, tiles_ref, side)
    out_ref[...] = acc_ref[...].astype(out_ref.dtype)


def last_hop(which, recvs, rows, owner, off, src, msg, tiles, width):
    _, feats, _ = msg.shape
    side = tiles.shape[1]
    half = pl.BlockSpec((feats // 2, width), lambda i, *_: (0, 0))
    return pl.pallas_call(
        functools.partial(last_kernel, which, side),
        out_shape=jax.ShapeDtypeStruct((feats, width), BF16),
        grid_spec=pltpu.PrefetchScalarGridSpec(
            num_scalar_prefetch=4,
            grid=(1,),
            in_specs=[half] * 4
            + [
                pl.BlockSpec(msg.shape, lambda i, *_: (0, 0, 0)),
                pl.BlockSpec(tiles.shape, lambda i, *_: (0, 0, 0)),
            ],
            out_specs=pl.BlockSpec((feats, width), lambda i, *_: (0, 0)),
            scratch_shapes=[pltpu.VMEM((feats, width), F32)],
        ),
        compiler_params=pltpu.CompilerParams(vmem_limit_bytes=VMEM_LIMIT),
        name="last_hop",
    )(rows, owner, off, src, *recvs, msg, tiles)


def back_kernel(side, owner, off, src, grads_ref, tiles_ref, *refs):
    out_ref, buf_ref, acc_ref, sem = refs[-4:]
    count = tiles_ref.shape[0]
    per_part = out_ref.shape[2] // side

    def fetch(t):
        at = pl.ds(pl.multiple_of(off[t] * side, side), side)
        return pltpu.make_async_copy(grads_ref.at[owner[t], :, at], buf_ref.at[t], sem.at[t])

    def begin(t, carry):
        fetch(t).start()
        return carry

    lax.fori_loop(0, count, begin, 0)
    acc_ref[...] = jnp.zeros_like(acc_ref)

    def step(t, carry):
        fetch(t).wait()
        term = jnp.dot(buf_ref[t], tiles_ref[t], preferred_element_type=F32)
        s = src[t]
        at = pl.ds(pl.multiple_of(lax.rem(s, per_part) * side, side), side)
        part = lax.div(s, per_part)
        acc_ref[part, :, at] = acc_ref[part, :, at] + term
        return carry

    lax.fori_loop(0, count, step, 0)
    out_ref[...] = acc_ref[...].astype(out_ref.dtype)


def back(owner, off, src, grads, tiles, parts, after):
    _, feats, width = grads.shape
    count, side, _ = tiles.shape
    shape = (parts, feats, width // parts)
    return pl.pallas_call(
        functools.partial(back_kernel, side),
        out_shape=jax.ShapeDtypeStruct(shape, BF16),
        grid_spec=pltpu.PrefetchScalarGridSpec(
            num_scalar_prefetch=3,
            grid=(1,),
            in_specs=[
                pl.BlockSpec(memory_space=pl.ANY),
                pl.BlockSpec(tiles.shape, lambda i, *_: (0, 0, 0)),
            ]
            + [pl.BlockSpec(memory_space=pl.ANY)] * len(after),
            out_specs=pl.BlockSpec(shape, lambda i, *_: (0, 0, 0)),
            scratch_shapes=[
                pltpu.VMEM((count, feats, side), BF16),
                pltpu.VMEM(shape, F32),
                pltpu.SemaphoreType.DMA((count,)),
            ],
        ),
        compiler_params=pltpu.CompilerParams(vmem_limit_bytes=VMEM_LIMIT),
        cost_estimate=pl.CostEstimate(
            flops=2 * feats * side * side * count, bytes_accessed=30 * 2**20, transcendentals=0
        ),
        name="back",
    )(owner, off, src, grads, tiles, *after)


def ring_device(
    node_feats,
    w_msg,
    step_table,
    step_ids,
    tile_vals,
    tile_owner,
    tile_dst_off,
    tile_src,
    cotangent,
):
    row_count = lax.axis_size("row")
    col_count = lax.axis_size("col")
    feats, width = cotangent.shape
    owner = tile_owner[:, 0]

    ring = ring_order(row_count)
    pos_of = np.argsort(np.array(ring))
    up = [(ring[p], ring[(p + 1) % row_count]) for p in range(row_count)]
    down = [(b, a) for a, b in up]
    far, near = row_count // 2, row_count - 1 - row_count // 2
    chains = [
        (0, 1, far),
        (0, -1, near),
        (1, 1, near),
        (1, -1, far),
    ]
    table = []
    for half, sign, hops in chains:
        for s in range(hops):
            table.append([ring[(pos_of[r] + sign * (hops - s)) % row_count] for r in range(row_count)])
    table.append(list(range(row_count)))
    table = jnp.asarray(np.array(table, dtype=np.int32).T)
    rows = lax.dynamic_index_in_dim(table, lax.axis_index("row"), 0, keepdims=False)

    grads = lax.all_gather(cotangent, "row", axis=0)

    step_hot = (
        step_ids[:, None] == jnp.arange(step_table.shape[0], dtype=jnp.int32)[None, :]
    ).astype(BF16)
    dims = (((0,), (1,)), ((), ()))
    pre_t = lax.dot_general(w_msg, node_feats, dims, preferred_element_type=F32)
    pre_t = pre_t + lax.dot_general(step_table, step_hot, dims, preferred_element_type=F32)
    msg_t = gelu_value(pre_t).astype(BF16)
    pre_t = lax.optimization_barrier(pre_t)
    nodes = msg_t.shape[1]
    msg = lax.all_to_all(
        msg_t.reshape(col_count, feats, nodes), "col", split_axis=0, concat_axis=0, tiled=True
    )

    held = [None] * len(chains)
    begun = []
    first = [sum(c[2] for c in chains[:i]) for i in range(len(chains))]
    for s in range(far):
        for i, (half, sign, hops) in enumerate(chains):
            skip = far - hops
            if s < skip:
                continue
            k = s - skip
            out = hop(
                first[i] + k, half, held[i], rows, owner, tile_dst_off, tile_src, msg, tile_vals, grads, width
            )
            if s == 0:
                begun.append(out)
            held[i] = lax.ppermute(out, "row", up if sign > 0 else down)
    which = sum(c[2] for c in chains)
    aggregated = last_hop(
        which, held, rows, owner, tile_dst_off, tile_src, msg, tile_vals, width
    )

    dmsg = back(owner, tile_dst_off, tile_src, grads, tile_vals, col_count, begun)
    return finish(node_feats, w_msg, pre_t, dmsg, aggregated)


GROUP = 4


def each_tile(meta, base, chip, product, add):
    low, high = meta[base + chip], meta[base + chip + 1]

    def step(g, carry):
        at = [low + g * GROUP + u for u in range(GROUP)]
        use = [jnp.minimum(i, high - 1) for i in at]
        parts = [product(i) for i in use]
        for i, j, part in zip(at, use, parts):
            add(j, jnp.where(i < high, part, 0.0))
        return carry

    lax.fori_loop(0, lax.div(high - low + GROUP - 1, GROUP), step, 0)


def parts_kernel(meta_own, meta_other, msg_own, msg_other, tiles_own, tiles_other, out_ref):
    count, side, _ = tiles_own.shape
    per_part = msg_own.shape[2] // side
    for q, (meta, msg, tiles) in enumerate(
        ((meta_own, msg_own, tiles_own), (meta_other, msg_other, tiles_other))
    ):

        def product(i, meta=meta, msg=msg, tiles=tiles):
            s = meta[2 * count + i]
            at = pl.ds(pl.multiple_of(lax.rem(s, per_part) * side, side), side)
            return lax.dot_general(
                msg[lax.div(s, per_part), :, at],
                tiles[meta[3 * count + i]],
                (((1,), (1,)), ((), ())),
                preferred_element_type=F32,
            )

        def step(g, carry, q=q, product=product):
            at = [g * GROUP + u for u in range(GROUP)]
            for i, part in zip(at, [product(i) for i in at]):
                out_ref[q, i] = part.astype(BF16)
            return carry

        lax.fori_loop(0, count // GROUP, step, 0)


SMEM = pl.BlockSpec(memory_space=pltpu.SMEM)
VMEM = pl.BlockSpec(memory_space=pltpu.VMEM)


def tile_parts(meta_own, meta_other, msg_own, msg_other, tiles_own, tiles_other):
    count, side, _ = tiles_own.shape
    feats = msg_own.shape[1]
    return pl.pallas_call(
        parts_kernel,
        out_shape=jax.ShapeDtypeStruct((2, count, feats, side), BF16),
        in_specs=[SMEM] * 2 + [VMEM] * 4,
        out_specs=VMEM,
        compiler_params=pltpu.CompilerParams(vmem_limit_bytes=PARTS_VMEM),
        cost_estimate=pl.CostEstimate(flops=2**30, bytes_accessed=12 * 2**20, transcendentals=0),
        name="tile_parts",
    )(meta_own, meta_other, msg_own, msg_other, tiles_own, tiles_other)


def sum_kernel(spec, ids, meta_own, meta_other, parts, *refs):
    chips, picks, low, split = spec
    recvs, rest = refs[: len(picks)], refs[len(picks) :]
    acc = rest[-1]
    outs = rest[:-1] if split else rest
    _, count, _, side = parts.shape
    feats = acc.shape[-2]
    base = 4 * count
    total = None
    for ref, pick in zip(recvs, picks):
        part = ref[...] if pick is None else ref[pick]
        part = part.reshape(acc.shape)
        if len(picks) > 1:
            part = part.astype(F32)
        total = part if total is None else total + part
    acc[...] = jnp.zeros_like(acc) if total is None else total.astype(acc.dtype)
    core = ids[ids.shape[0] - 1]
    for m, which in enumerate(chips):
        chip = ids[which]
        for q, meta in enumerate((meta_own, meta_other)):

            def step(i, carry, m=m, q=q, meta=meta):
                a = jnp.bitwise_xor(jnp.bitwise_and(meta[i], 1), core)
                at = (m, a) if len(chips) > 1 else (a,)
                to = pl.ds(pl.multiple_of(meta[count + i] * side, side), side)
                at = at + (slice(None), to)
                part = parts[q, i, low : low + feats, :].astype(F32)
                acc[at] = (acc[at].astype(F32) + part).astype(acc.dtype)
                return carry

            lax.fori_loop(meta[base + chip], meta[base + chip + 1], step, 0)
    if split:
        for a in (0, 1):
            outs[a][...] = acc[a].astype(BF16)


def tile_sums(env, chips, recvs, low, feats, width, split=False):
    ids, meta_own, meta_other, parts, _, _ = env
    shape = (2, feats, width) if len(chips) == 1 else (len(chips), 2, feats, width)
    if split:
        out = [jax.ShapeDtypeStruct((feats, width), BF16)] * 2
    else:
        out = jax.ShapeDtypeStruct(shape, BF16)
    spec = (tuple(chips), tuple(p for _, p in recvs), low, split)
    return pl.pallas_call(
        functools.partial(sum_kernel, spec),
        out_shape=out,
        in_specs=[SMEM] * 3 + [VMEM] * (1 + len(recvs)),
        out_specs=[VMEM] * 2 if split else VMEM,
        scratch_shapes=[pltpu.VMEM(shape, F32)] if split else [],
        compiler_params=pltpu.CompilerParams(vmem_limit_bytes=SMALL_VMEM),
        cost_estimate=pl.CostEstimate(flops=2**20, bytes_accessed=3 * 2**20, transcendentals=0),
        name="tile_sums",
    )(ids, meta_own, meta_other, parts, *[a for a, _ in recvs])


def grad_kernel(spec, ids, meta_own, meta_other, tiles_own, tiles_other, *refs):
    chips, has_sum, final = spec
    arrays, rest = refs[: len(chips)], refs[len(chips) :]
    count, side, _ = tiles_own.shape
    base = 4 * count
    if final:
        outs, acc = rest[-3:-1], rest[-1]
    else:
        acc = rest[-1]
    acc[...] = rest[0][...] if has_sum else jnp.zeros_like(acc)
    per_part = acc.shape[3] // side
    core = ids[ids.shape[0] - 1]
    for which, array in zip(chips, arrays):
        chip = ids[which]
        for q, (meta, tiles) in enumerate(((meta_own, tiles_own), (meta_other, tiles_other))):

            def product(i, meta=meta, tiles=tiles, array=array):
                a = jnp.bitwise_xor(jnp.bitwise_and(meta[i], 1), core)
                at = pl.ds(pl.multiple_of(meta[count + i] * side, side), side)
                return jnp.dot(
                    array[a, :, at], tiles[meta[3 * count + i]], preferred_element_type=F32
                )

            def add(i, term, q=q, meta=meta):
                s = meta[2 * count + i]
                part = lax.div(s, per_part)
                to = pl.ds(pl.multiple_of(lax.rem(s, per_part) * side, side), side)
                acc[q, part, :, to] = acc[q, part, :, to] + term

            each_tile(meta, base, chip, product, add)
    if final:
        for q in (0, 1):
            outs[q][...] = acc[q].astype(BF16)


def grad_sums(env, chips, arrays, so_far, parts, final):
    ids, meta_own, meta_other, _, tiles_own, tiles_other = env
    smem = pl.BlockSpec(memory_space=pltpu.SMEM)
    vmem = pl.BlockSpec(memory_space=pltpu.VMEM)
    _, feats, width = arrays[0].shape
    shape = (2, parts, feats, width // parts)
    if final:
        out = [jax.ShapeDtypeStruct(shape[1:], BF16)] * 2
        scratch = [pltpu.VMEM(shape, F32)]
    else:
        out = jax.ShapeDtypeStruct(shape, F32)
        scratch = []
    sums = [] if so_far is None else [so_far]
    return pl.pallas_call(
        functools.partial(grad_kernel, (tuple(chips), bool(sums), final)),
        out_shape=out,
        in_specs=[smem] * 3 + [vmem] * (2 + len(arrays) + len(sums)),
        out_specs=[vmem] * 2 if final else vmem,
        scratch_shapes=scratch,
        compiler_params=pltpu.CompilerParams(vmem_limit_bytes=GRID_VMEM),
        cost_estimate=pl.CostEstimate(flops=2**28, bytes_accessed=8 * 2**20, transcendentals=0),
        name="grad_sums",
    )(ids, meta_own, meta_other, tiles_own, tiles_other, *arrays, *sums)


def sorted_meta(owner, off, src, chips):
    count = owner.shape[0]
    key = owner // 2
    place = jnp.arange(count, dtype=jnp.int32)
    before = (key[None, :] < key[:, None]) | (
        (key[None, :] == key[:, None]) & (place[None, :] < place[:, None])
    )
    pos = jnp.sum(before.astype(jnp.int32), axis=1)
    hot = (pos[:, None] == place[None, :]).astype(jnp.int32)
    values = jnp.stack([owner, off, src, place])
    ordered = jnp.sum(values[:, :, None] * hot[None], axis=1)
    bounds = jnp.arange(chips + 2, dtype=jnp.int32)
    starts = jnp.sum((key[:, None] < bounds[None, :]).astype(jnp.int32), axis=0)
    return jnp.concatenate([ordered.reshape(-1), starts])


def grid_device(
    node_feats,
    w_msg,
    step_table,
    step_ids,
    tile_vals,
    tile_owner,
    tile_dst_off,
    tile_src,
    cotangent,
):
    row_count = lax.axis_size("row")
    col_count = lax.axis_size("col")
    feats, width = cotangent.shape
    slab = feats // 2
    feats_a = max(16, (3 * slab // 8) // 16 * 16)
    feats_b = slab - feats_a
    nz = row_count // 4
    chips = row_count // 2
    me = lax.axis_index("row")
    core = jnp.bitwise_and(me, 1)
    every = range(row_count)
    swap = [(r, r ^ 1) for r in every]

    def z_move(sign, ok):
        return [(r, r + 4 * sign) for r in every if 0 <= r // 4 + sign < nz and ok(r // 4)]

    def x_move(ok):
        return [(r, r ^ 2) for r in every if ok(r // 4)]

    def rel(dz, dx):
        return (dz + nz - 1) * 2 + dx

    def turn(j, dx):
        return (2 * nz - 1) * 2 + j * 2 + dx

    table = np.zeros((row_count, (2 * nz - 1) * 2 + 2 * nz + 1), np.int32)
    for r in every:
        z, x, c = r // 4, (r // 2) % 2, r % 2
        for dx in (0, 1):
            for dz in range(1 - nz, nz):
                inside = 0 <= z + dz < nz
                table[r, rel(dz, dx)] = (z + dz) * 2 + (x ^ dx) if inside else chips
            for j in range(nz):
                table[r, turn(j, dx)] = ((z + j) % nz) * 2 + (x ^ dx)
        table[r, -1] = c
    ids = lax.dynamic_index_in_dim(jnp.asarray(table), me, 0, keepdims=False)

    def permute(a, pairs):
        return lax.ppermute(a, "row", pairs)

    def mine_and_other(a, axis):
        size = a.shape[axis] // 2
        mine = lax.dynamic_slice_in_dim(a, core * size, size, axis)
        other = lax.dynamic_slice_in_dim(a, (1 - core) * size, size, axis)
        return mine, other

    def in_order(mine, other, axis):
        first = jnp.where(core == 0, mine, other)
        second = jnp.where(core == 0, other, mine)
        return jnp.concatenate([first, second], axis=axis)

    mine, other = mine_and_other(cotangent, 0)
    shard = jnp.stack([mine, permute(other, swap)])
    line = {0: shard}
    across = {0: permute(shard, x_move(lambda z: True))}
    for k in range(1, nz):
        for sign in (-1, 1):
            pairs = z_move(-sign, lambda z: 0 <= z + sign * (k - 1) < nz)
            line[sign * k] = permute(line[sign * (k - 1)], pairs)
        for sign in (-1, 1):
            pairs = x_move(lambda z: 0 <= z + sign * k < nz)
            across[sign * k] = permute(line[sign * k], pairs)

    meta_own = sorted_meta(tile_owner[:, 0], tile_dst_off, tile_src, chips)
    meta_other = permute(meta_own, swap)
    tiles_other = permute(tile_vals, swap)

    step_hot = (
        step_ids[:, None] == jnp.arange(step_table.shape[0], dtype=jnp.int32)[None, :]
    ).astype(BF16)
    dims = (((0,), (1,)), ((), ()))
    pre_t = lax.dot_general(w_msg, node_feats, dims, preferred_element_type=F32)
    pre_t = pre_t + lax.dot_general(step_table, step_hot, dims, preferred_element_type=F32)
    msg_t = gelu_value(pre_t).astype(BF16)
    pre_t = lax.optimization_barrier(pre_t)
    nodes = msg_t.shape[1]
    msg = lax.all_to_all(
        msg_t.reshape(col_count, feats, nodes), "col", split_axis=0, concat_axis=0, tiled=True
    )
    msg_own, other = mine_and_other(msg, 1)
    msg_other = permute(other, swap)
    parts = tile_parts(meta_own, meta_other, msg_own, msg_other, tile_vals, tiles_other)
    env = (ids, meta_own, meta_other, parts, tile_vals, tiles_other)

    def sums_a(chip, recvs, split=False):
        return tile_sums(env, [chip], recvs, 0, feats_a, width, split=split)

    def sums_b(picks, recvs, split=False):
        return tile_sums(env, picks, recvs, feats_a, feats_b, width, split=split)

    def known(a):
        return [] if a is None else [(a, None)]

    from_x = {j: permute(sums_a(turn(j, 1), []), x_move(lambda z: True)) for j in range(nz)}
    flow_a, flow_b = {-1: None, 1: None}, {-1: None, 1: None}
    for d in range(nz - 1, 0, -1):
        for sign in (1, -1):
            pairs = z_move(sign, lambda z: 0 <= z + sign * d < nz)
            out = sums_b([rel(sign * d, 0), rel(sign * d, 1)], known(flow_b[sign]))
            flow_b[sign] = permute(out, pairs)
            out = sums_a(rel(sign * d, 0), known(from_x[sign * d % nz]) + known(flow_a[sign]))
            flow_a[sign] = permute(out, pairs)
    recv_b = permute(sums_b([rel(0, 1)], [(flow_b[1], 1), (flow_b[-1], 1)]), x_move(lambda z: True))
    keep_b, send_b = sums_b(
        [rel(0, 0)], [(flow_b[1], 0), (flow_b[-1], 0), (recv_b, None)], split=True
    )
    keep_a, send_a = sums_a(
        rel(0, 0), known(from_x[0]) + known(flow_a[1]) + known(flow_a[-1]), split=True
    )
    other_a, other_b = permute(send_a, swap), permute(send_b, swap)
    aggregated = in_order(
        jnp.concatenate([keep_a, keep_b]), jnp.concatenate([other_a, other_b]), 0
    )

    def grads(dx, steps, so_far, final=False):
        arrays = [(line, across)[dx][dz] for dz in steps]
        return grad_sums(env, [rel(dz, dx) for dz in steps], arrays, so_far, col_count, final)

    near = [dz for dz in line if abs(dz) <= 1]
    far = [dz for dz in line if abs(dz) > 1]
    acc = grads(0, near, None)
    acc = grads(0, far, acc)
    acc = grads(1, near, acc)
    own, send = grads(1, far, acc, True)
    dmsg = in_order(own, permute(send, swap), 1)
    return finish(node_feats, w_msg, pre_t, dmsg, aggregated)


def finish(node_feats, w_msg, pre_t, dmsg, aggregated):
    dims = (((0,), (1,)), ((), ()))
    dmsg_rows = lax.all_to_all(dmsg, "col", split_axis=0, concat_axis=0, tiled=True)
    dmsg_rows = dmsg_rows.reshape(pre_t.shape)
    dpre_t = (dmsg_rows.astype(F32) * gelu_slope(pre_t)).astype(BF16)
    feat_grad = lax.dot_general(dpre_t, w_msg, dims, preferred_element_type=F32).astype(BF16)
    weight_term = lax.dot_general(
        node_feats, dpre_t, dims, preferred_element_type=F32
    ).astype(BF16)
    devices = lax.axis_size("row") * lax.axis_size("col")
    hidden = weight_term.shape[0]
    rows_each = hidden // devices
    axes = ("row", "col")
    shares = lax.all_to_all(
        weight_term.reshape(devices, rows_each, hidden), axes, split_axis=0, concat_axis=0, tiled=True
    )
    share = jnp.sum(shares.astype(F32), axis=0).astype(BF16)
    weight_grad = lax.all_to_all(
        jnp.broadcast_to(share[None], (devices,) + share.shape), axes, split_axis=0, concat_axis=0, tiled=True
    ).reshape(hidden, hidden)
    return (aggregated, feat_grad, weight_grad)


def solution(mesh):
    rows = mesh.shape["row"]
    in_grid = rows == 16

    def per_device(*args):
        return (grid_device if in_grid else ring_device)(*args)

    return jax.shard_map(
        per_device,
        mesh=mesh,
        in_specs=(
            P(("row", "col"), None),
            P(),
            P(),
            P(("row", "col")),
            P("row", None, None),
            P("row", None),
            P("row"),
            P("row"),
            P("col", "row"),
        ),
        out_specs=(P("col", "row"), P(("row", "col"), None), P()),
        check_vma=False,
    )
```

```python
import functools

import jax
import jax.numpy as jnp
import numpy as np
from jax import lax
from jax.experimental import pallas as pl
from jax.experimental.pallas import tpu as pltpu
from jax.sharding import PartitionSpec as P


F32 = jnp.float32
BF16 = jnp.bfloat16
VMEM_LIMIT = 48 * 1024 * 1024
GRID_VMEM = 32 * 1024 * 1024
PARTS_VMEM = 20 * 1024 * 1024
SMALL_VMEM = 16 * 1024 * 1024


def gelu_value(v):
    return 0.5 * v * (1.0 + jax.scipy.special.erf(v / jnp.sqrt(2.0)))


def gelu_slope(v):
    return 0.5 * (1.0 + jax.scipy.special.erf(v / jnp.sqrt(2.0))) + v * jnp.exp(
        -0.5 * v * v
    ) / jnp.sqrt(2.0 * jnp.pi)


def ring_order(row_count):
    chips = row_count // 2
    bits = max(chips.bit_length() - 1, 0)
    nz = 1 << ((bits + 1) // 2)
    nx = chips // nz
    path = []
    for x in range(nx):
        zs = range(1, nz) if x % 2 == 0 else range(nz - 1, 0, -1)
        if nz == 1:
            zs = range(0)
        path += [(z, x) for z in zs]
    path += [(0, x) for x in range(nx - 1, -1, -1)]
    order = []
    for z, x in path:
        order += [(z * nx + x) * 2, (z * nx + x) * 2 + 1]
    return order


def add_tiles(acc_ref, row, owner, off, src, msg_ref, tiles_ref, side):
    per_part = msg_ref.shape[2] // side

    def step(t, carry):
        @pl.when(owner[t] == row)
        def _():
            s = src[t]
            col = pl.multiple_of(lax.rem(s, per_part) * side, side)
            feats = msg_ref[lax.div(s, per_part), :, pl.ds(col, side)]
            part = lax.dot_general(
                feats, tiles_ref[t], (((1,), (1,)), ((), ())), preferred_element_type=F32
            )
            at = pl.ds(pl.multiple_of(off[t] * side, side), side)
            acc_ref[:, at] = acc_ref[:, at] + part

        return carry

    lax.fori_loop(0, tiles_ref.shape[0], step, 0)


def hop_kernel(which, has_recv, side, rows, owner, off, src, *refs):
    if has_recv:
        recv_ref, msg_ref, tiles_ref, _, out_ref, acc_ref = refs
        acc_ref[...] = recv_ref[...].astype(F32)
    else:
        msg_ref, tiles_ref, _, out_ref, acc_ref = refs
        acc_ref[...] = jnp.zeros_like(acc_ref)
    add_tiles(acc_ref, rows[which], owner, off, src, msg_ref, tiles_ref, side)
    out_ref[...] = acc_ref[...].astype(out_ref.dtype)


def hop(which, half, recv, rows, owner, off, src, msg, tiles, gate, width):
    parts, feats, part_nodes = msg.shape
    fh = feats // 2
    side = tiles.shape[1]
    args = ([recv] if recv is not None else []) + [msg, tiles, gate]
    vm = pl.BlockSpec(memory_space=pltpu.VMEM)
    full = pl.BlockSpec((fh, width), lambda i, *_: (0, 0))
    specs = ([full] if recv is not None else []) + [
        pl.BlockSpec((parts, fh, part_nodes), lambda i, *_: (0, half, 0)),
        pl.BlockSpec(tiles.shape, lambda i, *_: (0, 0, 0)),
        pl.BlockSpec(memory_space=pl.ANY),
    ]
    return pl.pallas_call(
        functools.partial(hop_kernel, which, recv is not None, side),
        out_shape=jax.ShapeDtypeStruct((fh, width), BF16),
        grid_spec=pltpu.PrefetchScalarGridSpec(
            num_scalar_prefetch=4,
            grid=(1,),
            in_specs=specs,
            out_specs=full,
            scratch_shapes=[pltpu.VMEM((fh, width), F32)],
        ),
        compiler_params=pltpu.CompilerParams(vmem_limit_bytes=VMEM_LIMIT),
        cost_estimate=pl.CostEstimate(
            flops=2 * fh * side * side * 9, bytes_accessed=6 * 2**20, transcendentals=0
        ),
        name="hop",
    )(rows, owner, off, src, *args)


def last_kernel(which, side, rows, owner, off, src, p0, m0, p1, m1, msg_ref, tiles_ref, out_ref, acc_ref):
    fh = p0.shape[0]
    acc_ref[:fh, :] = p0[...].astype(F32) + m0[...].astype(F32)
    acc_ref[fh:, :] = p1[...].astype(F32) + m1[...].astype(F32)
    add_tiles(acc_ref, rows[which], owner, off, src, msg_ref, tiles_ref, side)
    out_ref[...] = acc_ref[...].astype(out_ref.dtype)


def last_hop(which, recvs, rows, owner, off, src, msg, tiles, width):
    _, feats, _ = msg.shape
    side = tiles.shape[1]
    half = pl.BlockSpec((feats // 2, width), lambda i, *_: (0, 0))
    return pl.pallas_call(
        functools.partial(last_kernel, which, side),
        out_shape=jax.ShapeDtypeStruct((feats, width), BF16),
        grid_spec=pltpu.PrefetchScalarGridSpec(
            num_scalar_prefetch=4,
            grid=(1,),
            in_specs=[half] * 4
            + [
                pl.BlockSpec(msg.shape, lambda i, *_: (0, 0, 0)),
                pl.BlockSpec(tiles.shape, lambda i, *_: (0, 0, 0)),
            ],
            out_specs=pl.BlockSpec((feats, width), lambda i, *_: (0, 0)),
            scratch_shapes=[pltpu.VMEM((feats, width), F32)],
        ),
        compiler_params=pltpu.CompilerParams(vmem_limit_bytes=VMEM_LIMIT),
        name="last_hop",
    )(rows, owner, off, src, *recvs, msg, tiles)


def back_kernel(side, owner, off, src, grads_ref, tiles_ref, *refs):
    out_ref, buf_ref, acc_ref, sem = refs[-4:]
    count = tiles_ref.shape[0]
    per_part = out_ref.shape[2] // side

    def fetch(t):
        at = pl.ds(pl.multiple_of(off[t] * side, side), side)
        return pltpu.make_async_copy(grads_ref.at[owner[t], :, at], buf_ref.at[t], sem.at[t])

    def begin(t, carry):
        fetch(t).start()
        return carry

    lax.fori_loop(0, count, begin, 0)
    acc_ref[...] = jnp.zeros_like(acc_ref)

    def step(t, carry):
        fetch(t).wait()
        term = jnp.dot(buf_ref[t], tiles_ref[t], preferred_element_type=F32)
        s = src[t]
        at = pl.ds(pl.multiple_of(lax.rem(s, per_part) * side, side), side)
        part = lax.div(s, per_part)
        acc_ref[part, :, at] = acc_ref[part, :, at] + term
        return carry

    lax.fori_loop(0, count, step, 0)
    out_ref[...] = acc_ref[...].astype(out_ref.dtype)


def back(owner, off, src, grads, tiles, parts, after):
    _, feats, width = grads.shape
    count, side, _ = tiles.shape
    shape = (parts, feats, width // parts)
    return pl.pallas_call(
        functools.partial(back_kernel, side),
        out_shape=jax.ShapeDtypeStruct(shape, BF16),
        grid_spec=pltpu.PrefetchScalarGridSpec(
            num_scalar_prefetch=3,
            grid=(1,),
            in_specs=[
                pl.BlockSpec(memory_space=pl.ANY),
                pl.BlockSpec(tiles.shape, lambda i, *_: (0, 0, 0)),
            ]
            + [pl.BlockSpec(memory_space=pl.ANY)] * len(after),
            out_specs=pl.BlockSpec(shape, lambda i, *_: (0, 0, 0)),
            scratch_shapes=[
                pltpu.VMEM((count, feats, side), BF16),
                pltpu.VMEM(shape, F32),
                pltpu.SemaphoreType.DMA((count,)),
            ],
        ),
        compiler_params=pltpu.CompilerParams(vmem_limit_bytes=VMEM_LIMIT),
        cost_estimate=pl.CostEstimate(
            flops=2 * feats * side * side * count, bytes_accessed=30 * 2**20, transcendentals=0
        ),
        name="back",
    )(owner, off, src, grads, tiles, *after)


def ring_device(
    node_feats,
    w_msg,
    step_table,
    step_ids,
    tile_vals,
    tile_owner,
    tile_dst_off,
    tile_src,
    cotangent,
):
    row_count = lax.axis_size("row")
    col_count = lax.axis_size("col")
    feats, width = cotangent.shape
    owner = tile_owner[:, 0]

    ring = ring_order(row_count)
    pos_of = np.argsort(np.array(ring))
    up = [(ring[p], ring[(p + 1) % row_count]) for p in range(row_count)]
    down = [(b, a) for a, b in up]
    far, near = row_count // 2, row_count - 1 - row_count // 2
    chains = [
        (0, 1, far),
        (0, -1, near),
        (1, 1, near),
        (1, -1, far),
    ]
    table = []
    for half, sign, hops in chains:
        for s in range(hops):
            table.append([ring[(pos_of[r] + sign * (hops - s)) % row_count] for r in range(row_count)])
    table.append(list(range(row_count)))
    table = jnp.asarray(np.array(table, dtype=np.int32).T)
    rows = lax.dynamic_index_in_dim(table, lax.axis_index("row"), 0, keepdims=False)

    grads = lax.all_gather(cotangent, "row", axis=0)

    step_hot = (
        step_ids[:, None] == jnp.arange(step_table.shape[0], dtype=jnp.int32)[None, :]
    ).astype(BF16)
    dims = (((0,), (1,)), ((), ()))
    pre_t = lax.dot_general(w_msg, node_feats, dims, preferred_element_type=F32)
    pre_t = pre_t + lax.dot_general(step_table, step_hot, dims, preferred_element_type=F32)
    msg_t = gelu_value(pre_t).astype(BF16)
    pre_t = lax.optimization_barrier(pre_t)
    nodes = msg_t.shape[1]
    msg = lax.all_to_all(
        msg_t.reshape(col_count, feats, nodes), "col", split_axis=0, concat_axis=0, tiled=True
    )

    held = [None] * len(chains)
    begun = []
    first = [sum(c[2] for c in chains[:i]) for i in range(len(chains))]
    for s in range(far):
        for i, (half, sign, hops) in enumerate(chains):
            skip = far - hops
            if s < skip:
                continue
            k = s - skip
            out = hop(
                first[i] + k, half, held[i], rows, owner, tile_dst_off, tile_src, msg, tile_vals, grads, width
            )
            if s == 0:
                begun.append(out)
            held[i] = lax.ppermute(out, "row", up if sign > 0 else down)
    which = sum(c[2] for c in chains)
    aggregated = last_hop(
        which, held, rows, owner, tile_dst_off, tile_src, msg, tile_vals, width
    )

    dmsg = back(owner, tile_dst_off, tile_src, grads, tile_vals, col_count, begun)
    return finish(node_feats, w_msg, pre_t, dmsg, aggregated)


GROUP = 4


def each_tile(meta, base, chip, product, add):
    low, high = meta[base + chip], meta[base + chip + 1]

    def step(g, carry):
        at = [low + g * GROUP + u for u in range(GROUP)]
        use = [jnp.minimum(i, high - 1) for i in at]
        parts = [product(i) for i in use]
        for i, j, part in zip(at, use, parts):
            add(j, jnp.where(i < high, part, 0.0))
        return carry

    lax.fori_loop(0, lax.div(high - low + GROUP - 1, GROUP), step, 0)


def parts_kernel(meta_own, meta_other, msg_own, msg_other, tiles_own, tiles_other, out_ref):
    count, side, _ = tiles_own.shape
    per_part = msg_own.shape[2] // side
    for q, (meta, msg, tiles) in enumerate(
        ((meta_own, msg_own, tiles_own), (meta_other, msg_other, tiles_other))
    ):

        def product(i, meta=meta, msg=msg, tiles=tiles):
            s = meta[2 * count + i]
            at = pl.ds(pl.multiple_of(lax.rem(s, per_part) * side, side), side)
            return lax.dot_general(
                msg[lax.div(s, per_part), :, at],
                tiles[meta[3 * count + i]],
                (((1,), (1,)), ((), ())),
                preferred_element_type=F32,
            )

        def step(g, carry, q=q, product=product):
            at = [g * GROUP + u for u in range(GROUP)]
            for i, part in zip(at, [product(i) for i in at]):
                out_ref[q, i] = part.astype(BF16)
            return carry

        lax.fori_loop(0, count // GROUP, step, 0)


SMEM = pl.BlockSpec(memory_space=pltpu.SMEM)
VMEM = pl.BlockSpec(memory_space=pltpu.VMEM)


def tile_parts(meta_own, meta_other, msg_own, msg_other, tiles_own, tiles_other):
    count, side, _ = tiles_own.shape
    feats = msg_own.shape[1]
    return pl.pallas_call(
        parts_kernel,
        out_shape=jax.ShapeDtypeStruct((2, count, feats, side), BF16),
        in_specs=[SMEM] * 2 + [VMEM] * 4,
        out_specs=VMEM,
        compiler_params=pltpu.CompilerParams(vmem_limit_bytes=PARTS_VMEM),
        cost_estimate=pl.CostEstimate(flops=2**30, bytes_accessed=12 * 2**20, transcendentals=0),
        name="tile_parts",
    )(meta_own, meta_other, msg_own, msg_other, tiles_own, tiles_other)


def sum_kernel(spec, ids, meta_own, meta_other, parts, *refs):
    chips, picks, low, split = spec
    recvs, rest = refs[: len(picks)], refs[len(picks) :]
    acc = rest[-1]
    outs = rest[:-1] if split else rest
    _, count, _, side = parts.shape
    feats = acc.shape[-2]
    base = 4 * count
    total = None
    for ref, pick in zip(recvs, picks):
        part = ref[...] if pick is None else ref[pick]
        part = part.reshape(acc.shape)
        if len(picks) > 1:
            part = part.astype(F32)
        total = part if total is None else total + part
    acc[...] = jnp.zeros_like(acc) if total is None else total.astype(acc.dtype)
    core = ids[ids.shape[0] - 1]
    for m, which in enumerate(chips):
        chip = ids[which]
        for q, meta in enumerate((meta_own, meta_other)):

            def step(i, carry, m=m, q=q, meta=meta):
                a = jnp.bitwise_xor(jnp.bitwise_and(meta[i], 1), core)
                at = (m, a) if len(chips) > 1 else (a,)
                to = pl.ds(pl.multiple_of(meta[count + i] * side, side), side)
                at = at + (slice(None), to)
                part = parts[q, i, low : low + feats, :].astype(F32)
                acc[at] = (acc[at].astype(F32) + part).astype(acc.dtype)
                return carry

            lax.fori_loop(meta[base + chip], meta[base + chip + 1], step, 0)
    if split:
        for a in (0, 1):
            outs[a][...] = acc[a].astype(BF16)


def tile_sums(env, chips, recvs, low, feats, width, split=False):
    ids, meta_own, meta_other, parts, _, _ = env
    shape = (2, feats, width) if len(chips) == 1 else (len(chips), 2, feats, width)
    if split:
        out = [jax.ShapeDtypeStruct((feats, width), BF16)] * 2
    else:
        out = jax.ShapeDtypeStruct(shape, BF16)
    spec = (tuple(chips), tuple(p for _, p in recvs), low, split)
    return pl.pallas_call(
        functools.partial(sum_kernel, spec),
        out_shape=out,
        in_specs=[SMEM] * 3 + [VMEM] * (1 + len(recvs)),
        out_specs=[VMEM] * 2 if split else VMEM,
        scratch_shapes=[pltpu.VMEM(shape, F32)] if split else [],
        compiler_params=pltpu.CompilerParams(vmem_limit_bytes=SMALL_VMEM),
        cost_estimate=pl.CostEstimate(flops=2**20, bytes_accessed=3 * 2**20, transcendentals=0),
        name="tile_sums",
    )(ids, meta_own, meta_other, parts, *[a for a, _ in recvs])


def grad_kernel(spec, ids, meta_own, meta_other, tiles_own, tiles_other, *refs):
    chips, has_sum, final = spec
    arrays, rest = refs[: len(chips)], refs[len(chips) :]
    count, side, _ = tiles_own.shape
    base = 4 * count
    if final:
        outs, acc = rest[-3:-1], rest[-1]
    else:
        acc = rest[-1]
    acc[...] = rest[0][...] if has_sum else jnp.zeros_like(acc)
    per_part = acc.shape[3] // side
    core = ids[ids.shape[0] - 1]
    for which, array in zip(chips, arrays):
        chip = ids[which]
        for q, (meta, tiles) in enumerate(((meta_own, tiles_own), (meta_other, tiles_other))):

            def product(i, meta=meta, tiles=tiles, array=array):
                a = jnp.bitwise_xor(jnp.bitwise_and(meta[i], 1), core)
                at = pl.ds(pl.multiple_of(meta[count + i] * side, side), side)
                return jnp.dot(
                    array[a, :, at], tiles[meta[3 * count + i]], preferred_element_type=F32
                )

            def add(i, term, q=q, meta=meta):
                s = meta[2 * count + i]
                part = lax.div(s, per_part)
                to = pl.ds(pl.multiple_of(lax.rem(s, per_part) * side, side), side)
                acc[q, part, :, to] = acc[q, part, :, to] + term

            each_tile(meta, base, chip, product, add)
    if final:
        for q in (0, 1):
            outs[q][...] = acc[q].astype(BF16)


def grad_sums(env, chips, arrays, so_far, parts, final):
    ids, meta_own, meta_other, _, tiles_own, tiles_other = env
    smem = pl.BlockSpec(memory_space=pltpu.SMEM)
    vmem = pl.BlockSpec(memory_space=pltpu.VMEM)
    _, feats, width = arrays[0].shape
    shape = (2, parts, feats, width // parts)
    if final:
        out = [jax.ShapeDtypeStruct(shape[1:], BF16)] * 2
        scratch = [pltpu.VMEM(shape, F32)]
    else:
        out = jax.ShapeDtypeStruct(shape, F32)
        scratch = []
    sums = [] if so_far is None else [so_far]
    return pl.pallas_call(
        functools.partial(grad_kernel, (tuple(chips), bool(sums), final)),
        out_shape=out,
        in_specs=[smem] * 3 + [vmem] * (2 + len(arrays) + len(sums)),
        out_specs=[vmem] * 2 if final else vmem,
        scratch_shapes=scratch,
        compiler_params=pltpu.CompilerParams(vmem_limit_bytes=GRID_VMEM),
        cost_estimate=pl.CostEstimate(flops=2**28, bytes_accessed=8 * 2**20, transcendentals=0),
        name="grad_sums",
    )(ids, meta_own, meta_other, tiles_own, tiles_other, *arrays, *sums)


def sorted_meta(owner, off, src, chips):
    count = owner.shape[0]
    key = owner // 2
    place = jnp.arange(count, dtype=jnp.int32)
    before = (key[None, :] < key[:, None]) | (
        (key[None, :] == key[:, None]) & (place[None, :] < place[:, None])
    )
    pos = jnp.sum(before.astype(jnp.int32), axis=1)
    hot = (pos[:, None] == place[None, :]).astype(jnp.int32)
    values = jnp.stack([owner, off, src, place])
    ordered = jnp.sum(values[:, :, None] * hot[None], axis=1)
    bounds = jnp.arange(chips + 2, dtype=jnp.int32)
    starts = jnp.sum((key[:, None] < bounds[None, :]).astype(jnp.int32), axis=0)
    return jnp.concatenate([ordered.reshape(-1), starts])


def grid_device(
    node_feats,
    w_msg,
    step_table,
    step_ids,
    tile_vals,
    tile_owner,
    tile_dst_off,
    tile_src,
    cotangent,
):
    row_count = lax.axis_size("row")
    col_count = lax.axis_size("col")
    feats, width = cotangent.shape
    slab = feats // 2
    feats_a = max(16, (3 * slab // 8) // 16 * 16)
    feats_b = slab - feats_a
    nz = row_count // 4
    chips = row_count // 2
    me = lax.axis_index("row")
    core = jnp.bitwise_and(me, 1)
    every = range(row_count)
    swap = [(r, r ^ 1) for r in every]

    def z_move(sign, ok):
        return [(r, r + 4 * sign) for r in every if 0 <= r // 4 + sign < nz and ok(r // 4)]

    def x_move(ok):
        return [(r, r ^ 2) for r in every if ok(r // 4)]

    def rel(dz, dx):
        return (dz + nz - 1) * 2 + dx

    def turn(j, dx):
        return (2 * nz - 1) * 2 + j * 2 + dx

    table = np.zeros((row_count, (2 * nz - 1) * 2 + 2 * nz + 1), np.int32)
    for r in every:
        z, x, c = r // 4, (r // 2) % 2, r % 2
        for dx in (0, 1):
            for dz in range(1 - nz, nz):
                inside = 0 <= z + dz < nz
                table[r, rel(dz, dx)] = (z + dz) * 2 + (x ^ dx) if inside else chips
            for j in range(nz):
                table[r, turn(j, dx)] = ((z + j) % nz) * 2 + (x ^ dx)
        table[r, -1] = c
    ids = lax.dynamic_index_in_dim(jnp.asarray(table), me, 0, keepdims=False)

    def permute(a, pairs):
        return lax.ppermute(a, "row", pairs)

    def mine_and_other(a, axis):
        size = a.shape[axis] // 2
        mine = lax.dynamic_slice_in_dim(a, core * size, size, axis)
        other = lax.dynamic_slice_in_dim(a, (1 - core) * size, size, axis)
        return mine, other

    def in_order(mine, other, axis):
        first = jnp.where(core == 0, mine, other)
        second = jnp.where(core == 0, other, mine)
        return jnp.concatenate([first, second], axis=axis)

    mine, other = mine_and_other(cotangent, 0)
    shard = jnp.stack([mine, permute(other, swap)])
    line = {0: shard}
    across = {0: permute(shard, x_move(lambda z: True))}
    for k in range(1, nz):
        for sign in (-1, 1):
            pairs = z_move(-sign, lambda z: 0 <= z + sign * (k - 1) < nz)
            line[sign * k] = permute(line[sign * (k - 1)], pairs)
        for sign in (-1, 1):
            pairs = x_move(lambda z: 0 <= z + sign * k < nz)
            across[sign * k] = permute(line[sign * k], pairs)

    meta_own = sorted_meta(tile_owner[:, 0], tile_dst_off, tile_src, chips)
    meta_other = permute(meta_own, swap)
    tiles_other = permute(tile_vals, swap)

    step_hot = (
        step_ids[:, None] == jnp.arange(step_table.shape[0], dtype=jnp.int32)[None, :]
    ).astype(BF16)
    dims = (((0,), (1,)), ((), ()))
    pre_t = lax.dot_general(w_msg, node_feats, dims, preferred_element_type=F32)
    pre_t = pre_t + lax.dot_general(step_table, step_hot, dims, preferred_element_type=F32)
    msg_t = gelu_value(pre_t).astype(BF16)
    pre_t = lax.optimization_barrier(pre_t)
    nodes = msg_t.shape[1]
    msg = lax.all_to_all(
        msg_t.reshape(col_count, feats, nodes), "col", split_axis=0, concat_axis=0, tiled=True
    )
    msg_own, other = mine_and_other(msg, 1)
    msg_other = permute(other, swap)
    parts = tile_parts(meta_own, meta_other, msg_own, msg_other, tile_vals, tiles_other)
    env = (ids, meta_own, meta_other, parts, tile_vals, tiles_other)

    def sums_a(chip, recvs, split=False):
        return tile_sums(env, [chip], recvs, 0, feats_a, width, split=split)

    def sums_b(picks, recvs, split=False):
        return tile_sums(env, picks, recvs, feats_a, feats_b, width, split=split)

    def known(a):
        return [] if a is None else [(a, None)]

    from_x = {j: permute(sums_a(turn(j, 1), []), x_move(lambda z: True)) for j in range(nz)}
    flow_a, flow_b = {-1: None, 1: None}, {-1: None, 1: None}
    for d in range(nz - 1, 0, -1):
        for sign in (1, -1):
            pairs = z_move(sign, lambda z: 0 <= z + sign * d < nz)
            out = sums_b([rel(sign * d, 0), rel(sign * d, 1)], known(flow_b[sign]))
            flow_b[sign] = permute(out, pairs)
            out = sums_a(rel(sign * d, 0), known(from_x[sign * d % nz]) + known(flow_a[sign]))
            flow_a[sign] = permute(out, pairs)
    recv_b = permute(sums_b([rel(0, 1)], [(flow_b[1], 1), (flow_b[-1], 1)]), x_move(lambda z: True))
    keep_b, send_b = sums_b(
        [rel(0, 0)], [(flow_b[1], 0), (flow_b[-1], 0), (recv_b, None)], split=True
    )
    keep_a, send_a = sums_a(
        rel(0, 0), known(from_x[0]) + known(flow_a[1]) + known(flow_a[-1]), split=True
    )
    other_a, other_b = permute(send_a, swap), permute(send_b, swap)
    aggregated = in_order(
        jnp.concatenate([keep_a, keep_b]), jnp.concatenate([other_a, other_b]), 0
    )

    def grads(steps, so_far, final=False):
        arrays = [(line, across)[dx][dz] for dx, dz in steps]
        return grad_sums(env, [rel(dz, dx) for dx, dz in steps], arrays, so_far, col_count, final)

    def both(dx, *steps):
        return [(dx, sign * k) for k in steps for sign in (-1, 1)]

    acc = grads([(0, 0)] + both(0, 1), None)
    acc = grads([(1, 0)] + both(0, 2), acc)
    acc = grads(both(1, 1) + both(0, *range(3, nz)), acc)
    own, send = grads(both(1, *range(2, nz)), acc, True)
    dmsg = in_order(own, permute(send, swap), 1)
    return finish(node_feats, w_msg, pre_t, dmsg, aggregated)


def finish(node_feats, w_msg, pre_t, dmsg, aggregated):
    dims = (((0,), (1,)), ((), ()))
    dmsg_rows = lax.all_to_all(dmsg, "col", split_axis=0, concat_axis=0, tiled=True)
    dmsg_rows = dmsg_rows.reshape(pre_t.shape)
    dpre_t = (dmsg_rows.astype(F32) * gelu_slope(pre_t)).astype(BF16)
    feat_grad = lax.dot_general(dpre_t, w_msg, dims, preferred_element_type=F32).astype(BF16)
    weight_term = lax.dot_general(
        node_feats, dpre_t, dims, preferred_element_type=F32
    ).astype(BF16)
    devices = lax.axis_size("row") * lax.axis_size("col")
    hidden = weight_term.shape[0]
    rows_each = hidden // devices
    axes = ("row", "col")
    shares = lax.all_to_all(
        weight_term.reshape(devices, rows_each, hidden), axes, split_axis=0, concat_axis=0, tiled=True
    )
    share = jnp.sum(shares.astype(F32), axis=0).astype(BF16)
    weight_grad = lax.all_to_all(
        jnp.broadcast_to(share[None], (devices,) + share.shape), axes, split_axis=0, concat_axis=0, tiled=True
    ).reshape(hidden, hidden)
    return (aggregated, feat_grad, weight_grad)


def solution(mesh):
    rows = mesh.shape["row"]
    in_grid = rows == 16

    def per_device(*args):
        return (grid_device if in_grid else ring_device)(*args)

    return jax.shard_map(
        per_device,
        mesh=mesh,
        in_specs=(
            P(("row", "col"), None),
            P(),
            P(),
            P(("row", "col")),
            P("row", None, None),
            P("row", None),
            P("row"),
            P("row"),
            P("col", "row"),
        ),
        out_specs=(P("col", "row"), P(("row", "col"), None), P()),
        check_vma=False,
    )
```

```python
import functools

import jax
import jax.numpy as jnp
import numpy as np
from jax import lax
from jax.experimental import pallas as pl
from jax.experimental.pallas import tpu as pltpu
from jax.sharding import PartitionSpec as P


F32 = jnp.float32
BF16 = jnp.bfloat16
VMEM_LIMIT = 48 * 1024 * 1024
GRID_VMEM = 24 * 1024 * 1024
PARTS_VMEM = 16 * 1024 * 1024
SMALL_VMEM = 10 * 1024 * 1024


def gelu_value(v):
    return 0.5 * v * (1.0 + jax.scipy.special.erf(v / jnp.sqrt(2.0)))


def gelu_slope(v):
    return 0.5 * (1.0 + jax.scipy.special.erf(v / jnp.sqrt(2.0))) + v * jnp.exp(
        -0.5 * v * v
    ) / jnp.sqrt(2.0 * jnp.pi)


def ring_order(row_count):
    chips = row_count // 2
    bits = max(chips.bit_length() - 1, 0)
    nz = 1 << ((bits + 1) // 2)
    nx = chips // nz
    path = []
    for x in range(nx):
        zs = range(1, nz) if x % 2 == 0 else range(nz - 1, 0, -1)
        if nz == 1:
            zs = range(0)
        path += [(z, x) for z in zs]
    path += [(0, x) for x in range(nx - 1, -1, -1)]
    order = []
    for z, x in path:
        order += [(z * nx + x) * 2, (z * nx + x) * 2 + 1]
    return order


def add_tiles(acc_ref, row, owner, off, src, msg_ref, tiles_ref, side):
    per_part = msg_ref.shape[2] // side

    def step(t, carry):
        @pl.when(owner[t] == row)
        def _():
            s = src[t]
            col = pl.multiple_of(lax.rem(s, per_part) * side, side)
            feats = msg_ref[lax.div(s, per_part), :, pl.ds(col, side)]
            part = lax.dot_general(
                feats, tiles_ref[t], (((1,), (1,)), ((), ())), preferred_element_type=F32
            )
            at = pl.ds(pl.multiple_of(off[t] * side, side), side)
            acc_ref[:, at] = acc_ref[:, at] + part

        return carry

    lax.fori_loop(0, tiles_ref.shape[0], step, 0)


def hop_kernel(which, has_recv, side, rows, owner, off, src, *refs):
    if has_recv:
        recv_ref, msg_ref, tiles_ref, _, out_ref, acc_ref = refs
        acc_ref[...] = recv_ref[...].astype(F32)
    else:
        msg_ref, tiles_ref, _, out_ref, acc_ref = refs
        acc_ref[...] = jnp.zeros_like(acc_ref)
    add_tiles(acc_ref, rows[which], owner, off, src, msg_ref, tiles_ref, side)
    out_ref[...] = acc_ref[...].astype(out_ref.dtype)


def hop(which, half, recv, rows, owner, off, src, msg, tiles, gate, width):
    parts, feats, part_nodes = msg.shape
    fh = feats // 2
    side = tiles.shape[1]
    args = ([recv] if recv is not None else []) + [msg, tiles, gate]
    vm = pl.BlockSpec(memory_space=pltpu.VMEM)
    full = pl.BlockSpec((fh, width), lambda i, *_: (0, 0))
    specs = ([full] if recv is not None else []) + [
        pl.BlockSpec((parts, fh, part_nodes), lambda i, *_: (0, half, 0)),
        pl.BlockSpec(tiles.shape, lambda i, *_: (0, 0, 0)),
        pl.BlockSpec(memory_space=pl.ANY),
    ]
    return pl.pallas_call(
        functools.partial(hop_kernel, which, recv is not None, side),
        out_shape=jax.ShapeDtypeStruct((fh, width), BF16),
        grid_spec=pltpu.PrefetchScalarGridSpec(
            num_scalar_prefetch=4,
            grid=(1,),
            in_specs=specs,
            out_specs=full,
            scratch_shapes=[pltpu.VMEM((fh, width), F32)],
        ),
        compiler_params=pltpu.CompilerParams(vmem_limit_bytes=VMEM_LIMIT),
        cost_estimate=pl.CostEstimate(
            flops=2 * fh * side * side * 9, bytes_accessed=6 * 2**20, transcendentals=0
        ),
        name="hop",
    )(rows, owner, off, src, *args)


def last_kernel(which, side, rows, owner, off, src, p0, m0, p1, m1, msg_ref, tiles_ref, out_ref, acc_ref):
    fh = p0.shape[0]
    acc_ref[:fh, :] = p0[...].astype(F32) + m0[...].astype(F32)
    acc_ref[fh:, :] = p1[...].astype(F32) + m1[...].astype(F32)
    add_tiles(acc_ref, rows[which], owner, off, src, msg_ref, tiles_ref, side)
    out_ref[...] = acc_ref[...].astype(out_ref.dtype)


def last_hop(which, recvs, rows, owner, off, src, msg, tiles, width):
    _, feats, _ = msg.shape
    side = tiles.shape[1]
    half = pl.BlockSpec((feats // 2, width), lambda i, *_: (0, 0))
    return pl.pallas_call(
        functools.partial(last_kernel, which, side),
        out_shape=jax.ShapeDtypeStruct((feats, width), BF16),
        grid_spec=pltpu.PrefetchScalarGridSpec(
            num_scalar_prefetch=4,
            grid=(1,),
            in_specs=[half] * 4
            + [
                pl.BlockSpec(msg.shape, lambda i, *_: (0, 0, 0)),
                pl.BlockSpec(tiles.shape, lambda i, *_: (0, 0, 0)),
            ],
            out_specs=pl.BlockSpec((feats, width), lambda i, *_: (0, 0)),
            scratch_shapes=[pltpu.VMEM((feats, width), F32)],
        ),
        compiler_params=pltpu.CompilerParams(vmem_limit_bytes=VMEM_LIMIT),
        name="last_hop",
    )(rows, owner, off, src, *recvs, msg, tiles)


def back_kernel(side, owner, off, src, grads_ref, tiles_ref, *refs):
    out_ref, buf_ref, acc_ref, sem = refs[-4:]
    count = tiles_ref.shape[0]
    per_part = out_ref.shape[2] // side

    def fetch(t):
        at = pl.ds(pl.multiple_of(off[t] * side, side), side)
        return pltpu.make_async_copy(grads_ref.at[owner[t], :, at], buf_ref.at[t], sem.at[t])

    def begin(t, carry):
        fetch(t).start()
        return carry

    lax.fori_loop(0, count, begin, 0)
    acc_ref[...] = jnp.zeros_like(acc_ref)

    def step(t, carry):
        fetch(t).wait()
        term = jnp.dot(buf_ref[t], tiles_ref[t], preferred_element_type=F32)
        s = src[t]
        at = pl.ds(pl.multiple_of(lax.rem(s, per_part) * side, side), side)
        part = lax.div(s, per_part)
        acc_ref[part, :, at] = acc_ref[part, :, at] + term
        return carry

    lax.fori_loop(0, count, step, 0)
    out_ref[...] = acc_ref[...].astype(out_ref.dtype)


def back(owner, off, src, grads, tiles, parts, after):
    _, feats, width = grads.shape
    count, side, _ = tiles.shape
    shape = (parts, feats, width // parts)
    return pl.pallas_call(
        functools.partial(back_kernel, side),
        out_shape=jax.ShapeDtypeStruct(shape, BF16),
        grid_spec=pltpu.PrefetchScalarGridSpec(
            num_scalar_prefetch=3,
            grid=(1,),
            in_specs=[
                pl.BlockSpec(memory_space=pl.ANY),
                pl.BlockSpec(tiles.shape, lambda i, *_: (0, 0, 0)),
            ]
            + [pl.BlockSpec(memory_space=pl.ANY)] * len(after),
            out_specs=pl.BlockSpec(shape, lambda i, *_: (0, 0, 0)),
            scratch_shapes=[
                pltpu.VMEM((count, feats, side), BF16),
                pltpu.VMEM(shape, F32),
                pltpu.SemaphoreType.DMA((count,)),
            ],
        ),
        compiler_params=pltpu.CompilerParams(vmem_limit_bytes=VMEM_LIMIT),
        cost_estimate=pl.CostEstimate(
            flops=2 * feats * side * side * count, bytes_accessed=30 * 2**20, transcendentals=0
        ),
        name="back",
    )(owner, off, src, grads, tiles, *after)


def ring_device(
    node_feats,
    w_msg,
    step_table,
    step_ids,
    tile_vals,
    tile_owner,
    tile_dst_off,
    tile_src,
    cotangent,
):
    row_count = lax.axis_size("row")
    col_count = lax.axis_size("col")
    feats, width = cotangent.shape
    owner = tile_owner[:, 0]

    ring = ring_order(row_count)
    pos_of = np.argsort(np.array(ring))
    up = [(ring[p], ring[(p + 1) % row_count]) for p in range(row_count)]
    down = [(b, a) for a, b in up]
    far, near = row_count // 2, row_count - 1 - row_count // 2
    chains = [
        (0, 1, far),
        (0, -1, near),
        (1, 1, near),
        (1, -1, far),
    ]
    table = []
    for half, sign, hops in chains:
        for s in range(hops):
            table.append([ring[(pos_of[r] + sign * (hops - s)) % row_count] for r in range(row_count)])
    table.append(list(range(row_count)))
    table = jnp.asarray(np.array(table, dtype=np.int32).T)
    rows = lax.dynamic_index_in_dim(table, lax.axis_index("row"), 0, keepdims=False)

    grads = lax.all_gather(cotangent, "row", axis=0)

    step_hot = (
        step_ids[:, None] == jnp.arange(step_table.shape[0], dtype=jnp.int32)[None, :]
    ).astype(BF16)
    dims = (((0,), (1,)), ((), ()))
    pre_t = lax.dot_general(w_msg, node_feats, dims, preferred_element_type=F32)
    pre_t = pre_t + lax.dot_general(step_table, step_hot, dims, preferred_element_type=F32)
    msg_t = gelu_value(pre_t).astype(BF16)
    pre_t = lax.optimization_barrier(pre_t)
    nodes = msg_t.shape[1]
    msg = lax.all_to_all(
        msg_t.reshape(col_count, feats, nodes), "col", split_axis=0, concat_axis=0, tiled=True
    )

    held = [None] * len(chains)
    begun = []
    first = [sum(c[2] for c in chains[:i]) for i in range(len(chains))]
    for s in range(far):
        for i, (half, sign, hops) in enumerate(chains):
            skip = far - hops
            if s < skip:
                continue
            k = s - skip
            out = hop(
                first[i] + k, half, held[i], rows, owner, tile_dst_off, tile_src, msg, tile_vals, grads, width
            )
            if s == 0:
                begun.append(out)
            held[i] = lax.ppermute(out, "row", up if sign > 0 else down)
    which = sum(c[2] for c in chains)
    aggregated = last_hop(
        which, held, rows, owner, tile_dst_off, tile_src, msg, tile_vals, width
    )

    dmsg = back(owner, tile_dst_off, tile_src, grads, tile_vals, col_count, begun)
    return finish(node_feats, w_msg, pre_t, dmsg, aggregated)


GROUP = 4
PARTS_GROUP = 8


def each_tile(meta, base, chip, product, add):
    low, high = meta[base + chip], meta[base + chip + 1]

    def step(g, carry):
        at = [low + g * GROUP + u for u in range(GROUP)]
        use = [jnp.minimum(i, high - 1) for i in at]
        parts = [product(i) for i in use]
        for i, j, part in zip(at, use, parts):
            add(j, jnp.where(i < high, part, 0.0))
        return carry

    lax.fori_loop(0, lax.div(high - low + GROUP - 1, GROUP), step, 0)


def parts_kernel(meta_own, meta_other, msg_own, msg_other, tiles_own, tiles_other, out_ref):
    count, side, _ = tiles_own.shape
    per_part = msg_own.shape[2] // side
    for q, (meta, msg, tiles) in enumerate(
        ((meta_own, msg_own, tiles_own), (meta_other, msg_other, tiles_other))
    ):

        def product(i, meta=meta, msg=msg, tiles=tiles):
            s = meta[2 * count + i]
            at = pl.ds(pl.multiple_of(lax.rem(s, per_part) * side, side), side)
            return lax.dot_general(
                msg[lax.div(s, per_part), :, at],
                tiles[meta[3 * count + i]],
                (((1,), (1,)), ((), ())),
                preferred_element_type=F32,
            )

        def step(g, carry, q=q, product=product):
            at = [g * PARTS_GROUP + u for u in range(PARTS_GROUP)]
            for i, part in zip(at, [product(i) for i in at]):
                out_ref[q, i] = part.astype(BF16)
            return carry

        lax.fori_loop(0, count // PARTS_GROUP, step, 0)


SMEM = pl.BlockSpec(memory_space=pltpu.SMEM)
VMEM = pl.BlockSpec(memory_space=pltpu.VMEM)


def tile_parts(meta_own, meta_other, msg_own, msg_other, tiles_own, tiles_other):
    count, side, _ = tiles_own.shape
    feats = msg_own.shape[1]
    return pl.pallas_call(
        parts_kernel,
        out_shape=jax.ShapeDtypeStruct((2, count, feats, side), BF16),
        in_specs=[SMEM] * 2 + [VMEM] * 4,
        out_specs=VMEM,
        compiler_params=pltpu.CompilerParams(vmem_limit_bytes=PARTS_VMEM),
        cost_estimate=pl.CostEstimate(flops=2**30, bytes_accessed=12 * 2**20, transcendentals=0),
        name="tile_parts",
    )(meta_own, meta_other, msg_own, msg_other, tiles_own, tiles_other)


def sum_kernel(spec, ids, meta_own, meta_other, parts, *refs):
    chips, picks, low, split = spec
    recvs, rest = refs[: len(picks)], refs[len(picks) :]
    acc = rest[-1]
    outs = rest[:-1] if split else rest
    _, count, _, side = parts.shape
    feats = acc.shape[-2]
    base = 4 * count
    total = None
    for ref, pick in zip(recvs, picks):
        part = ref[...] if pick is None else ref[pick]
        part = part.reshape(acc.shape)
        if len(picks) > 1:
            part = part.astype(F32)
        total = part if total is None else total + part
    acc[...] = jnp.zeros_like(acc) if total is None else total.astype(acc.dtype)
    core = ids[ids.shape[0] - 1]
    for m, which in enumerate(chips):
        chip = ids[which]
        for q, meta in enumerate((meta_own, meta_other)):

            def step(i, carry, m=m, q=q, meta=meta):
                a = jnp.bitwise_xor(jnp.bitwise_and(meta[i], 1), core)
                at = (m, a) if len(chips) > 1 else (a,)
                to = pl.ds(pl.multiple_of(meta[count + i] * side, side), side)
                at = at + (slice(None), to)
                part = parts[q, i, low : low + feats, :].astype(F32)
                acc[at] = (acc[at].astype(F32) + part).astype(acc.dtype)
                return carry

            lax.fori_loop(meta[base + chip], meta[base + chip + 1], step, 0)
    if split:
        for a in (0, 1):
            outs[a][...] = acc[a].astype(BF16)


def tile_sums(env, chips, recvs, low, feats, width, split=False):
    ids, meta_own, meta_other, parts, _, _ = env
    shape = (2, feats, width) if len(chips) == 1 else (len(chips), 2, feats, width)
    if split:
        out = [jax.ShapeDtypeStruct((feats, width), BF16)] * 2
    else:
        out = jax.ShapeDtypeStruct(shape, BF16)
    spec = (tuple(chips), tuple(p for _, p in recvs), low, split)
    return pl.pallas_call(
        functools.partial(sum_kernel, spec),
        out_shape=out,
        in_specs=[SMEM] * 3 + [VMEM] * (1 + len(recvs)),
        out_specs=[VMEM] * 2 if split else VMEM,
        scratch_shapes=[pltpu.VMEM(shape, F32)] if split else [],
        compiler_params=pltpu.CompilerParams(vmem_limit_bytes=SMALL_VMEM),
        cost_estimate=pl.CostEstimate(flops=2**20, bytes_accessed=3 * 2**20, transcendentals=0),
        name="tile_sums",
    )(ids, meta_own, meta_other, parts, *[a for a, _ in recvs])


def grad_kernel(spec, ids, meta_own, meta_other, tiles_own, tiles_other, *refs):
    chips, has_sum, final = spec
    arrays, rest = refs[: len(chips)], refs[len(chips) :]
    count, side, _ = tiles_own.shape
    base = 4 * count
    if final:
        outs, acc = rest[-3:-1], rest[-1]
    else:
        acc = rest[-1]
    acc[...] = rest[0][...] if has_sum else jnp.zeros_like(acc)
    per_part = acc.shape[3] // side
    core = ids[ids.shape[0] - 1]
    for which, array in zip(chips, arrays):
        chip = ids[which]
        for q, (meta, tiles) in enumerate(((meta_own, tiles_own), (meta_other, tiles_other))):

            def product(i, meta=meta, tiles=tiles, array=array):
                a = jnp.bitwise_xor(jnp.bitwise_and(meta[i], 1), core)
                at = pl.ds(pl.multiple_of(meta[count + i] * side, side), side)
                return jnp.dot(
                    array[a, :, at], tiles[meta[3 * count + i]], preferred_element_type=F32
                )

            def add(i, term, q=q, meta=meta):
                s = meta[2 * count + i]
                part = lax.div(s, per_part)
                to = pl.ds(pl.multiple_of(lax.rem(s, per_part) * side, side), side)
                acc[q, part, :, to] = acc[q, part, :, to] + term

            each_tile(meta, base, chip, product, add)
    if final:
        for q in (0, 1):
            outs[q][...] = acc[q].astype(BF16)


def grad_sums(env, chips, arrays, so_far, parts, final):
    ids, meta_own, meta_other, _, tiles_own, tiles_other = env
    smem = pl.BlockSpec(memory_space=pltpu.SMEM)
    vmem = pl.BlockSpec(memory_space=pltpu.VMEM)
    _, feats, width = arrays[0].shape
    shape = (2, parts, feats, width // parts)
    if final:
        out = [jax.ShapeDtypeStruct(shape[1:], BF16)] * 2
        scratch = [pltpu.VMEM(shape, F32)]
    else:
        out = jax.ShapeDtypeStruct(shape, F32)
        scratch = []
    sums = [] if so_far is None else [so_far]
    return pl.pallas_call(
        functools.partial(grad_kernel, (tuple(chips), bool(sums), final)),
        out_shape=out,
        in_specs=[smem] * 3 + [vmem] * (2 + len(arrays) + len(sums)),
        out_specs=[vmem] * 2 if final else vmem,
        scratch_shapes=scratch,
        compiler_params=pltpu.CompilerParams(vmem_limit_bytes=GRID_VMEM),
        cost_estimate=pl.CostEstimate(flops=2**28, bytes_accessed=8 * 2**20, transcendentals=0),
        name="grad_sums",
    )(ids, meta_own, meta_other, tiles_own, tiles_other, *arrays, *sums)


def sorted_meta(owner, off, src, chips):
    count = owner.shape[0]
    key = owner // 2
    place = jnp.arange(count, dtype=jnp.int32)
    before = (key[None, :] < key[:, None]) | (
        (key[None, :] == key[:, None]) & (place[None, :] < place[:, None])
    )
    pos = jnp.sum(before.astype(jnp.int32), axis=1)
    hot = (pos[:, None] == place[None, :]).astype(jnp.int32)
    values = jnp.stack([owner, off, src, place])
    ordered = jnp.sum(values[:, :, None] * hot[None], axis=1)
    bounds = jnp.arange(chips + 2, dtype=jnp.int32)
    starts = jnp.sum((key[:, None] < bounds[None, :]).astype(jnp.int32), axis=0)
    return jnp.concatenate([ordered.reshape(-1), starts])


def grid_device(
    node_feats,
    w_msg,
    step_table,
    step_ids,
    tile_vals,
    tile_owner,
    tile_dst_off,
    tile_src,
    cotangent,
):
    row_count = lax.axis_size("row")
    col_count = lax.axis_size("col")
    feats, width = cotangent.shape
    slab = feats // 2
    feats_a = max(16, (3 * slab // 8) // 16 * 16)
    feats_b = slab - feats_a
    nz = row_count // 4
    chips = row_count // 2
    me = lax.axis_index("row")
    core = jnp.bitwise_and(me, 1)
    every = range(row_count)
    swap = [(r, r ^ 1) for r in every]

    def z_move(sign, ok):
        return [(r, r + 4 * sign) for r in every if 0 <= r // 4 + sign < nz and ok(r // 4)]

    def x_move(ok):
        return [(r, r ^ 2) for r in every if ok(r // 4)]

    def rel(dz, dx):
        return (dz + nz - 1) * 2 + dx

    def turn(j, dx):
        return (2 * nz - 1) * 2 + j * 2 + dx

    table = np.zeros((row_count, (2 * nz - 1) * 2 + 2 * nz + 1), np.int32)
    for r in every:
        z, x, c = r // 4, (r // 2) % 2, r % 2
        for dx in (0, 1):
            for dz in range(1 - nz, nz):
                inside = 0 <= z + dz < nz
                table[r, rel(dz, dx)] = (z + dz) * 2 + (x ^ dx) if inside else chips
            for j in range(nz):
                table[r, turn(j, dx)] = ((z + j) % nz) * 2 + (x ^ dx)
        table[r, -1] = c
    ids = lax.dynamic_index_in_dim(jnp.asarray(table), me, 0, keepdims=False)

    def permute(a, pairs):
        return lax.ppermute(a, "row", pairs)

    def mine_and_other(a, axis):
        size = a.shape[axis] // 2
        mine = lax.dynamic_slice_in_dim(a, core * size, size, axis)
        other = lax.dynamic_slice_in_dim(a, (1 - core) * size, size, axis)
        return mine, other

    def in_order(mine, other, axis):
        first = jnp.where(core == 0, mine, other)
        second = jnp.where(core == 0, other, mine)
        return jnp.concatenate([first, second], axis=axis)

    mine, other = mine_and_other(cotangent, 0)
    shard = jnp.stack([mine, permute(other, swap)])
    line = {0: shard}
    across = {0: permute(shard, x_move(lambda z: True))}
    for k in range(1, nz):
        for sign in (-1, 1):
            pairs = z_move(-sign, lambda z: 0 <= z + sign * (k - 1) < nz)
            line[sign * k] = permute(line[sign * (k - 1)], pairs)
        for sign in (-1, 1):
            pairs = x_move(lambda z: 0 <= z + sign * k < nz)
            across[sign * k] = permute(line[sign * k], pairs)

    meta_own = sorted_meta(tile_owner[:, 0], tile_dst_off, tile_src, chips)
    meta_other = permute(meta_own, swap)
    tiles_other = permute(tile_vals, swap)

    step_hot = (
        step_ids[:, None] == jnp.arange(step_table.shape[0], dtype=jnp.int32)[None, :]
    ).astype(BF16)
    dims = (((0,), (1,)), ((), ()))
    pre_t = lax.dot_general(w_msg, node_feats, dims, preferred_element_type=F32)
    pre_t = pre_t + lax.dot_general(step_table, step_hot, dims, preferred_element_type=F32)
    msg_t = gelu_value(pre_t).astype(BF16)
    pre_t = lax.optimization_barrier(pre_t)
    nodes = msg_t.shape[1]
    msg = lax.all_to_all(
        msg_t.reshape(col_count, feats, nodes), "col", split_axis=0, concat_axis=0, tiled=True
    )
    msg_own, other = mine_and_other(msg, 1)
    msg_other = permute(other, swap)
    parts = tile_parts(meta_own, meta_other, msg_own, msg_other, tile_vals, tiles_other)
    env = (ids, meta_own, meta_other, parts, tile_vals, tiles_other)

    def sums_a(chip, recvs, split=False):
        return tile_sums(env, [chip], recvs, 0, feats_a, width, split=split)

    def sums_b(picks, recvs, split=False):
        return tile_sums(env, picks, recvs, feats_a, feats_b, width, split=split)

    def known(a):
        return [] if a is None else [(a, None)]

    from_x = {j: permute(sums_a(turn(j, 1), []), x_move(lambda z: True)) for j in range(nz)}
    flow_a, flow_b = {-1: None, 1: None}, {-1: None, 1: None}
    for d in range(nz - 1, 0, -1):
        for sign in (1, -1):
            pairs = z_move(sign, lambda z: 0 <= z + sign * d < nz)
            out = sums_b([rel(sign * d, 0), rel(sign * d, 1)], known(flow_b[sign]))
            flow_b[sign] = permute(out, pairs)
            out = sums_a(rel(sign * d, 0), known(from_x[sign * d % nz]) + known(flow_a[sign]))
            flow_a[sign] = permute(out, pairs)
    recv_b = permute(sums_b([rel(0, 1)], [(flow_b[1], 1), (flow_b[-1], 1)]), x_move(lambda z: True))
    keep_b, send_b = sums_b(
        [rel(0, 0)], [(flow_b[1], 0), (flow_b[-1], 0), (recv_b, None)], split=True
    )
    keep_a, send_a = sums_a(
        rel(0, 0), known(from_x[0]) + known(flow_a[1]) + known(flow_a[-1]), split=True
    )
    other_a, other_b = permute(send_a, swap), permute(send_b, swap)
    aggregated = in_order(
        jnp.concatenate([keep_a, keep_b]), jnp.concatenate([other_a, other_b]), 0
    )

    def grads(steps, so_far, final=False):
        arrays = [(line, across)[dx][dz] for dx, dz in steps]
        return grad_sums(env, [rel(dz, dx) for dx, dz in steps], arrays, so_far, col_count, final)

    def both(dx, *steps):
        return [(dx, sign * k) for k in steps for sign in (-1, 1)]

    acc = grads([(0, 0)] + both(0, 1), None)
    acc = grads([(1, 0)] + both(0, 2), acc)
    acc = grads(both(1, 1) + both(0, *range(3, nz)), acc)
    own, send = grads(both(1, *range(2, nz)), acc, True)
    dmsg = in_order(own, permute(send, swap), 1)
    return finish(node_feats, w_msg, pre_t, dmsg, aggregated)


def finish(node_feats, w_msg, pre_t, dmsg, aggregated):
    dims = (((0,), (1,)), ((), ()))
    dmsg_rows = lax.all_to_all(dmsg, "col", split_axis=0, concat_axis=0, tiled=True)
    dmsg_rows = dmsg_rows.reshape(pre_t.shape)
    dpre_t = (dmsg_rows.astype(F32) * gelu_slope(pre_t)).astype(BF16)
    feat_grad = lax.dot_general(dpre_t, w_msg, dims, preferred_element_type=F32).astype(BF16)
    weight_term = lax.dot_general(
        node_feats, dpre_t, dims, preferred_element_type=F32
    ).astype(BF16)
    devices = lax.axis_size("row") * lax.axis_size("col")
    hidden = weight_term.shape[0]
    rows_each = hidden // devices
    axes = ("row", "col")
    shares = lax.all_to_all(
        weight_term.reshape(devices, rows_each, hidden), axes, split_axis=0, concat_axis=0, tiled=True
    )
    share = jnp.sum(shares.astype(F32), axis=0).astype(BF16)
    weight_grad = lax.all_to_all(
        jnp.broadcast_to(share[None], (devices,) + share.shape), axes, split_axis=0, concat_axis=0, tiled=True
    ).reshape(hidden, hidden)
    return (aggregated, feat_grad, weight_grad)


def solution(mesh):
    rows = mesh.shape["row"]
    in_grid = rows == 16

    def per_device(*args):
        return (grid_device if in_grid else ring_device)(*args)

    return jax.shard_map(
        per_device,
        mesh=mesh,
        in_specs=(
            P(("row", "col"), None),
            P(),
            P(),
            P(("row", "col")),
            P("row", None, None),
            P("row", None),
            P("row"),
            P("row"),
            P("col", "row"),
        ),
        out_specs=(P("col", "row"), P(("row", "col"), None), P()),
        check_vma=False,
    )
```
